32 devices in a mesh: expert: 8 (over z, y), replica: 4 (over x, core).
Axes of the slice: x: 2, y: 2, z: 4, core: 2. Of those that a mesh axis runs over, the one named last changes fastest.
Arguments:
- tokens: bfloat16 [2048, 2880], P(('expert', 'replica')), may hold values from -6 to 6
- expert_ids: int32 [2048, 4], P(('expert', 'replica')), may hold values from 0 to 7, all different within a row; in each aligned block of 64 rows (0 to 63, 64 to 127, ...) at most 48 rows name the same one
- gate_codes: int32 [2048, 4], P(('expert', 'replica')), may hold values from 1 to 65535
- w_gate: bfloat16 [8, 2880, 2880], P('expert', None, 'replica'), may hold values from -0.109375 to 0.109375
- w_up: bfloat16 [8, 2880, 2880], P('expert', None, 'replica'), may hold values from -0.109375 to 0.109375
- w_down: bfloat16 [8, 2880, 2880], P('expert', 'replica'), may hold values from -0.109375 to 0.109375
Outputs:
- mixed: bfloat16 [2048, 2880], P(('expert', 'replica'))
The draws below stay inside these ranges and needn't reach their ends.
Inputs may be any that keep to these rules, and one draw needn't show every extreme that they name: `expert_ids`: each row names 4 different experts. Among the 64 rows of one device each expert is named at most 48 times, a bound that some block reaches.
All inputs are finite; a program needn't handle non-finite values.
Results may differ from the reference program's by a relative error of at most 0.015.
Values may be sent and summed in bfloat16 or wider, within the bound.
A program may use at most 128 MiB of HBM per device.

```python
import math
import jax
import jax.numpy as jnp
import numpy as np
from jax import lax

D = 2880
FF = 2880
TOP = 4
TOK_DEV = 64
EXPERTS = 8
CAP = 48
TOKENS = 2048
N_EXPERT = 8
N_REPLICA = 4


def with_ends(entries, stream_key, smallest, largest):
    index_at = [jax.random.randint(jax.random.fold_in(stream_key, axis), (), 0, length) for axis, length in enumerate(entries.shape)]
    longest = entries.shape.index(max(entries.shape))
    next_to = index_at[:longest] + [(index_at[longest] + 1) % entries.shape[longest]] + index_at[longest + 1:]
    return entries.at[tuple(index_at)].set(smallest).at[tuple(next_to)].set(largest)


def block_levels(key, extent, shards, low, top_value):
    level, own = 1.0, jax.random.fold_in(key, 6)
    for position, blocks in shards:
        draws = jnp.exp(jax.random.uniform(jax.random.fold_in(own, position), (blocks,), jnp.float32, low / len(shards), top_value / len(shards)))
        level = level * jnp.repeat(draws, extent[position] // blocks).reshape([-1 if axis == position else 1 for axis in range(len(extent))])
    return level


def deal_out(stream_key, own, number, rows, number_of, top, reach, lean):
    order = jax.random.permutation(stream_key, number_of)
    crowded, usual = shares(number_of, rows * top, reach, lean, True), shares(number_of, rows * top, reach, lean, False)
    places = jnp.arange(number_of)

    def named(sizes, turn):
        used = int((sizes > 0).sum())
        fixed = max(1, used // 4)
        passed = fixed + (places - fixed + turn * (used - fixed)) % max(1, number_of - fixed)
        return jnp.zeros((number_of,), jnp.int32).at[order[jnp.where(places < fixed, places, passed)]].set(jnp.asarray(sizes, jnp.int32))

    sizes = jnp.where(number % 4 == 0, named(crowded, number // 4), named(usual, number - number // 4 - 1))
    mixed = jax.random.permutation(jax.random.fold_in(own, 3), number_of)
    donor, receiver = mixed[0:number_of // 2 * 2:2], mixed[1:number_of // 2 * 2:2]
    margin = jnp.minimum(sizes[donor] - 1, reach - sizes[receiver]) // 2
    margin = jnp.where((donor == order[0]) | (receiver == order[0]) | (sizes[receiver] == 0), 0, jnp.maximum(margin, 0))
    passed = jax.random.randint(jax.random.fold_in(own, 4), (number_of // 2,), 0, 1 << 20) % (margin + 1)
    sizes = sizes.at[donor].add(-passed).at[receiver].add(passed)
    items = jnp.searchsorted(jnp.cumsum(sizes), jnp.arange(rows * top), side="right").astype(jnp.int32)
    listing = items.reshape(top, rows).T
    listing = listing[jax.random.permutation(jax.random.fold_in(own, 1), rows)]
    turn = jax.random.randint(jax.random.fold_in(own, 2), (rows, 1), 0, top)
    return jnp.take_along_axis(listing, (jnp.arange(top)[None, :] + turn) % top, axis=1)


def shares(amount, total, reach, slope, full):
    loads = [(1 << 20) // math.isqrt(standing ** slope) + 1 for standing in range(1, amount + 1)]
    largest = reach if full else min(reach, max(-(-total // amount), total * loads[0] // sum(loads)))
    least = 1 if total - largest >= amount - 1 else 0
    given, spare = [largest] + [least] * (amount - 1), total - largest - least * (amount - 1)
    while spare > 0:
        free = [i for i in range(1, amount) if given[i] < largest] or [i for i in range(1, amount) if given[i] < reach]
        whole, remaining = sum([loads[i] for i in free]), spare
        for i in free:
            addition = min(reach - given[i], max(1, remaining * loads[i] // whole), spare)
            given[i] = given[i] + addition
            spare = spare - addition
    return np.array(given)


def centred(stream_key, extent, width, reach, pieces=(), held_as=jnp.bfloat16):
    array = width * jax.random.normal(stream_key, extent, jnp.float32)
    if pieces:
        array = array * block_levels(stream_key, extent, pieces, -0.22, 0.18)
    return jnp.clip(array, -reach, reach).astype(held_as)


def setup_inputs(seed: int = 0) -> dict:
    arg_keys = jax.random.split(jax.random.key(seed), 7)
    tokens = centred(arg_keys[0], (TOKENS, D), 1.0, 6.0, ((0, 32),))
    expert_ids_keys = jax.random.split(jax.random.fold_in(arg_keys[1], 1), TOKENS // TOK_DEV)
    expert_ids_turns = jax.random.permutation(jax.random.fold_in(arg_keys[1], 3), TOKENS // TOK_DEV)
    expert_ids = jax.vmap(lambda own, number: deal_out(jax.random.fold_in(arg_keys[1], 2), own, number, TOK_DEV, EXPERTS, TOP, CAP, 2))(expert_ids_keys, expert_ids_turns).reshape((TOKENS, TOP))
    gate_codes = with_ends(jax.random.randint(arg_keys[2], (TOKENS, TOP), 1, 65536), jax.random.fold_in(arg_keys[2], 1), 1, 65535).astype(jnp.int32)
    w_gate = centred(arg_keys[3], (EXPERTS, D, FF), D ** -0.5, 0.109375, ((0, 8), (2, 4)))
    w_up = centred(arg_keys[4], (EXPERTS, D, FF), D ** -0.5, 0.109375, ((0, 8), (2, 4)))
    w_down = centred(arg_keys[5], (EXPERTS, FF, D), FF ** -0.5, 0.109375, ((0, 8), (1, 4)))
    return {"tokens": tokens, "expert_ids": expert_ids, "gate_codes": gate_codes, "w_gate": w_gate, "w_up": w_up, "w_down": w_down}


def activate(gate, up):
    return gate * jax.nn.sigmoid(1.702 * gate) * (up + 1.0)


def reference(tokens, expert_ids, gate_codes, w_gate, w_up, w_down):
    count_rows = tokens.shape[0]
    flat_ids = expert_ids.reshape(-1)
    gates = gate_codes.reshape(-1).astype(jnp.float32) / 65536.0
    most_rows = N_EXPERT * N_REPLICA * CAP
    part_width = FF // N_REPLICA

    def one_expert(expert, total):
        chosen = flat_ids == expert
        count = jnp.sum(chosen.astype(jnp.int32))
        where = jnp.nonzero(chosen, size=most_rows, fill_value=0)[0].astype(jnp.int32)
        valid = (jnp.arange(most_rows, dtype=jnp.int32) < count).astype(jnp.float32)
        owner = (where // TOP).astype(jnp.int32)
        rows = tokens[owner]
        gate = jnp.dot(rows, w_gate[expert], preferred_element_type=jnp.float32)
        up = jnp.dot(rows, w_up[expert], preferred_element_type=jnp.float32)
        hidden = activate(gate, up).astype(jnp.bfloat16)
        result = jnp.zeros((most_rows, D), jnp.float32)
        for part in range(N_REPLICA):
            piece = jnp.dot(hidden[:, part * part_width:(part + 1) * part_width],
                            w_down[expert, part * part_width:(part + 1) * part_width],
                            preferred_element_type=jnp.float32).astype(jnp.bfloat16)
            piece = lax.optimization_barrier(piece)
            result = result + piece.astype(jnp.float32)
        rounded = lax.optimization_barrier(result.astype(jnp.bfloat16))
        weight = gates[where] * valid
        return total.at[owner].add(rounded.astype(jnp.float32) * weight[:, None])

    total = lax.fori_loop(0, EXPERTS, one_expert, jnp.zeros((count_rows, D), jnp.float32))
    return total.astype(jnp.bfloat16)
```

```python
import functools

import jax
import jax.numpy as jnp
from jax import lax
from jax.experimental import pallas as pl
from jax.experimental.pallas import tpu as pltpu
from jax.sharding import PartitionSpec as P

MESH = pl.DeviceIdType.MESH
CORES = 2


def activate(gate, up):
    return gate * jax.nn.sigmoid(1.702 * gate) * (up + 1.0)


def spans(extent, step):
    return [(low, min(low + step, extent)) for low in range(0, extent, step)]


def fused(
    depth, experts, cap, cut_in, cut_mid, cut_out, plan,
    tokens, ids, codes, w_gate, w_up, w_down, out,
    tok, far_tok, meta, far_meta, y_pick, x_buf, wg, wu, wd, hid, part, c_in,
    x_out, x_in, y_out, y_in, z_out, z_in, acc, w_sem,
    zt_s, zt_r, zf_s, zf_r, m_s, m_r, fm_s, fm_r, fx_s, raw_s, raw_r,
    ya_s, ya_r, yb_s, yb_r, xa_s, xa_r, xb_s, xb_r, c_s, c_r,
    pc_s, pc_r, pxa_s, pxa_r, pxb_s, pxb_r, pya_s, pya_r, pyb_s, pyb_r,
    pza_s, pza_r, pzb_s, pzb_r,
):
    rows, width = tokens.shape
    f32, bf16 = jnp.float32, jnp.bfloat16
    expert, replica = lax.axis_index("expert"), lax.axis_index("replica")
    z, y = expert // 2, expert % 2
    other = z * 2 + (1 - y)
    x_side = (replica + CORES) % (2 * CORES)
    y_peer = {"expert": other}
    x_peer = {"replica": x_side}
    c_peer = {"replica": replica // CORES * CORES + (1 - replica % CORES)}
    near, wide, rest = pl.ds(0, cut_in), pl.ds(cut_in, width - cut_in), pl.ds(cut_mid, width - cut_mid)
    mid = pl.ds(cut_in, cut_mid - cut_in)
    first, second = pl.ds(0, cut_out), pl.ds(cut_out, width - cut_out)
    group = 2 * cap

    def z_peer(level):
        return {"expert": level * 2 + y}

    def ahead(step):
        return (z + step) % depth

    def send(src, dst, ssem, rsem, peer):
        pltpu.make_async_remote_copy(
            src_ref=src, dst_ref=dst, send_sem=ssem, recv_sem=rsem,
            device_id=peer, device_id_type=MESH,
        ).start()

    def arrived(dst, sem):
        pltpu.make_async_copy(dst, dst, sem).wait()

    def block_at(i):
        pairs = jnp.minimum(z, depth - 1 - z)
        inward = jnp.where(2 * z < depth, 1, -1)
        beside = jnp.where(i % 2 == 1, z + inward * ((i + 1) // 2), z - inward * (i // 2))
        beyond = jnp.where(2 * z < depth, i, depth - 1 - i)
        return jnp.where(i <= 2 * pairs, beside, beyond)

    barrier = pltpu.get_barrier_semaphore()
    greeted = [y_peer, x_peer, c_peer]
    for step in range(1, depth):
        greeted.append(z_peer(ahead(step)))
    for peer in greeted:
        pl.semaphore_signal(barrier, inc=1, device_id=peer, device_id_type=MESH)
    own_load = pltpu.make_async_copy(tokens, tok.at[z], zt_r.at[z])
    own_load.start()
    loads = [
        pltpu.make_async_copy(src.at[0], dst, w_sem.at[i])
        for i, (src, dst) in enumerate(((w_gate, wg), (w_up, wu), (w_down, wd)))
    ]
    for load in loads:
        load.start()

    label = lax.broadcasted_iota(jnp.int32, (experts, rows), 0)
    named = jnp.zeros((experts, rows), f32)
    weight = jnp.zeros((experts, rows), f32)
    for k in range(ids.shape[0]):
        same = label == ids[k : k + 1, :]
        named = named + jnp.where(same, 1.0, 0.0)
        weight = weight + jnp.where(same, codes[k : k + 1, :].astype(f32) / 65536.0, 0.0)
    upto = lax.broadcasted_iota(jnp.int32, (rows, rows), 0) <= lax.broadcasted_iota(
        jnp.int32, (rows, rows), 1
    )
    counts = jnp.dot(
        named.astype(bf16), jnp.where(upto, 1.0, 0.0).astype(bf16), preferred_element_type=f32
    )
    meta[z, pl.ds(0, experts), :] = jnp.where(named > 0, counts - 1.0, -1.0)
    meta[z, pl.ds(experts, experts), :] = weight

    pl.semaphore_wait(barrier, len(greeted))
    own_load.wait()

    def pass_on(s, src, ssem, rsem):
        @pl.when((s <= z) & (z < depth - 1))
        def _():
            send(src, src, ssem.at[0, s], rsem.at[s], z_peer(ahead(1)))

        @pl.when((s >= z) & (z > 0))
        def _():
            send(src, src, ssem.at[1, s], rsem.at[s], z_peer(ahead(depth - 1)))

    def passed(s, src, ssem):
        @pl.when((s <= z) & (z < depth - 1))
        def _():
            arrived(src, ssem.at[0, s])

        @pl.when((s >= z) & (z > 0))
        def _():
            arrived(src, ssem.at[1, s])

    between = (z > 0) & (z < depth - 1)
    pass_on(z, meta.at[z], m_s, m_r)
    pass_on(z, tok.at[z], zt_s, zt_r)
    send(meta.at[z], far_meta.at[z], fx_s.at[0], fm_r.at[z], x_peer)
    send(tok.at[z, :, wide], far_tok.at[z, :, wide], raw_s.at[z], raw_r.at[z], x_peer)

    def row_of(table, which):
        sub = lax.broadcasted_iota(jnp.int32, table.shape, 0)
        return jnp.sum(jnp.where(sub == which, table, 0.0), axis=0, keepdims=True)

    def slots(table, which):
        slot = lax.broadcasted_iota(jnp.int32, (cap, rows), 0).astype(f32)
        return slot == row_of(table, which)

    def picker(table):
        return jnp.concatenate(
            [jnp.where(slots(table, e), 1.0, 0.0) for e in (expert, other)], axis=0
        ).astype(bf16)

    def spreader(table):
        high, low = [], []
        for e in (expert, other):
            share = row_of(table, e + experts)
            coarse = share.astype(bf16).astype(f32)
            here = slots(table, e)
            high.append(jnp.where(here, coarse, 0.0))
            low.append(jnp.where(here, share - coarse, 0.0))
        return jnp.concatenate(high + low, axis=0).astype(bf16)

    def spread(matrix, own, far):
        stacked = jnp.concatenate([own, far, own, far], axis=0)
        return lax.dot_general(
            matrix, stacked, (((0,), (0,)), ((), ())), preferred_element_type=f32
        )

    def relay(i):
        s = block_at(i)

        @pl.when(between)
        def _():
            arrived(meta.at[s], m_r.at[s])
            pass_on(s, meta.at[s], m_s, m_r)
            arrived(tok.at[s], zt_r.at[s])
            pass_on(s, tok.at[s], zt_s, zt_r)

    def relay_far(i):
        s = block_at(i)

        @pl.when(between)
        def _():
            arrived(far_meta.at[s], fm_r.at[s])
            pass_on(s, far_meta.at[s], fm_s, fm_r)
            if cut_mid < width:
                arrived(far_tok.at[s, :, rest], zf_r.at[s])
                pass_on(s, far_tok.at[s, :, rest], zf_s, zf_r)

    def choose(i):
        s = block_at(i)

        @pl.when((i > 0) & jnp.logical_not(between))
        def _():
            arrived(meta.at[s], m_r.at[s])
            arrived(tok.at[s], zt_r.at[s])

        if cut_mid > cut_in:
            @pl.when(i > 0)
            def _():
                send(tok.at[s, :, mid], far_tok.at[s, :, mid], raw_s.at[s], raw_r.at[s], x_peer)

        chosen = jnp.dot(picker(meta[s]), tok[s], preferred_element_type=f32).astype(bf16)
        x_buf[s, pl.ds(0, cap), :] = chosen[:cap]
        y_pick[s, pl.ds(0, cap), :] = chosen[cap:]
        send(y_pick.at[s, pl.ds(0, cap), near], x_buf.at[s, pl.ds(group, cap), near],
             ya_s.at[s], ya_r.at[s], y_peer)
        send(x_buf.at[s, pl.ds(0, cap), near], x_buf.at[s, pl.ds(cap, cap), near],
             xa_s.at[s], xa_r.at[s], x_peer)

    def choose_far(i):
        s = block_at(i)

        @pl.when(i == 0)
        def _():
            arrived(far_meta.at[s], fm_r.at[s])
            pass_on(s, far_meta.at[s], fm_s, fm_r)
            arrived(far_tok.at[s, :, wide], raw_r.at[s])
            if cut_mid < width:
                pass_on(s, far_tok.at[s, :, rest], zf_s, zf_r)

        @pl.when((i > 0) & jnp.logical_not(between))
        def _():
            arrived(far_meta.at[s], fm_r.at[s])
            if cut_mid < width:
                arrived(far_tok.at[s, :, rest], zf_r.at[s])

        if cut_mid > cut_in:
            @pl.when(i > 0)
            def _():
                arrived(far_tok.at[s, :, mid], raw_r.at[s])

        chosen = jnp.dot(
            picker(far_meta[s]), far_tok[s, :, wide], preferred_element_type=f32
        ).astype(bf16)
        x_buf[s, pl.ds(cap, cap), wide] = chosen[:cap]
        y_pick[s, pl.ds(cap, cap), wide] = chosen[cap:]
        send(y_pick.at[s, :, wide], x_buf.at[s, pl.ds(group, group), wide],
             yb_s.at[s], yb_r.at[s], y_peer)

    def forward(i):
        s = block_at(i)
        here = x_buf.at[s, pl.ds(group, cap), near]
        arrived(here, ya_r.at[s])
        send(here, x_buf.at[s, pl.ds(group + cap, cap), near], xb_s.at[s], xb_r.at[s], x_peer)

    def to_core(i):
        s = block_at(i)
        arrived(x_buf.at[s, pl.ds(cap, cap), near], xa_r.at[s])
        arrived(x_buf.at[s, pl.ds(group, group), wide], yb_r.at[s])
        arrived(x_buf.at[s, pl.ds(group + cap, cap), near], xb_r.at[s])
        send(x_buf.at[s, pl.ds(0, 2 * group)], x_buf.at[s, pl.ds(2 * group, 2 * group)],
             c_s.at[s], c_r.at[s], c_peer)

    def ffn_up(i):
        s = block_at(i)
        arrived(c_in.at[s], c_r.at[s])

        @pl.when(i == 0)
        def _():
            for load in loads:
                load.wait()

        across = (((1,), (1,)), ((), ()))
        for low, high in spans(wg.shape[0], 256):
            block = x_buf[s]
            gate = lax.dot_general(block, wg[low:high, :], across, preferred_element_type=f32)
            up = lax.dot_general(block, wu[low:high, :], across, preferred_element_type=f32)
            hid[:, low:high] = activate(gate, up).astype(bf16)

    def ffn_down(i):
        s = block_at(i)
        for low, high in spans(width, 512):
            part[s, :, low:high] = jnp.dot(
                hid[...], wd[:, low:high], preferred_element_type=f32
            ).astype(bf16)
        send(part.at[s, pl.ds(2 * group, 2 * group)], c_in.at[s], pc_s.at[s], pc_r.at[s], c_peer)

    def pair(s, low, count, cols):
        return part[s, pl.ds(low, count), cols].astype(f32) + c_in[s, pl.ds(low, count), cols].astype(f32)

    def sum_core(j):
        s = block_at(j)
        arrived(c_in.at[s], pc_r.at[s])
        for n in range(2):
            x_out[s, pl.ds(n * cap, cap), first] = pair(s, cap + n * group, cap, first).astype(bf16)
        send(x_out.at[s, :, first], x_in.at[s, :, first], pxa_s.at[s], pxa_r.at[s], x_peer)
        y_out[s, :, second] = pair(s, group, group, second).astype(bf16)
        send(y_out.at[s, :, second], y_in.at[s, :, second], pyb_s.at[s], pyb_r.at[s], y_peer)

    def sum_x(j):
        s = block_at(j)
        arrived(x_in.at[s, :, first], pxa_r.at[s])
        y_out[s, pl.ds(0, cap), first] = (
            pair(s, group, cap, first) + x_in[s, pl.ds(cap, cap), first].astype(f32)
        ).astype(bf16)
        send(y_out.at[s, pl.ds(0, cap), first], y_in.at[s, pl.ds(0, cap), first],
             pya_s.at[s], pya_r.at[s], y_peer)

    def sum_y(j):
        s = block_at(j)
        arrived(y_in.at[s, :, second], pyb_r.at[s])
        x_out[s, pl.ds(0, rows), second] = spread(
            spreader(far_meta[s]), pair(s, cap, cap, second).astype(bf16), y_in[s, pl.ds(cap, cap), second]
        ).astype(bf16)
        send(x_out.at[s, pl.ds(0, rows), second], x_in.at[s, pl.ds(0, rows), second],
             pxb_s.at[s], pxb_r.at[s], x_peer)

    def comb_a(j):
        s = block_at(j)
        arrived(y_in.at[s, pl.ds(0, cap), first], pya_r.at[s])
        own = (pair(s, 0, cap, first) + x_in[s, pl.ds(0, cap), first].astype(f32)).astype(bf16)
        total = spread(spreader(meta[s]), own, y_in[s, pl.ds(0, cap), first])

        @pl.when(s == z)
        def _():
            acc[:, first] = total

        @pl.when(s != z)
        def _():
            z_out[s, :, first] = total.astype(bf16)
            send(z_out.at[s, :, first], z_in.at[z, :, first], pza_s.at[s], pza_r.at[z], z_peer(s))

    def comb_b(j):
        s = block_at(j)
        arrived(x_in.at[s, pl.ds(0, rows), second], pxb_r.at[s])
        total = spread(
            spreader(meta[s]), pair(s, 0, cap, second).astype(bf16), y_in[s, pl.ds(0, cap), second]
        ) + x_in[s, pl.ds(0, rows), second].astype(f32)

        @pl.when(s == z)
        def _():
            acc[:, second] = total

        @pl.when(s != z)
        def _():
            z_out[s, :, second] = total.astype(bf16)
            send(z_out.at[s, :, second], z_in.at[z, :, second], pzb_s.at[s], pzb_r.at[z], z_peer(s))

    table = {
        "relay": relay, "relay_far": relay_far, "choose": choose, "choose_far": choose_far,
        "forward": forward, "to_core": to_core, "ffn_up": ffn_up, "ffn_down": ffn_down,
        "sum_core": sum_core, "sum_x": sum_x, "sum_y": sum_y, "comb_a": comb_a, "comb_b": comb_b,
    }

    def tick(t, carry):
        for name, starts in plan:
            hit, i = t < 0, 0
            for k, start in enumerate(starts):
                if start is not None:
                    hit = hit | (t == start)
                    i = jnp.where(t == start, k, i)

            @pl.when(hit)
            def _():
                table[name](i)
        return carry

    ticks = 1 + max(start for _, starts in plan for start in starts if start is not None)
    lax.fori_loop(0, ticks, tick, 0)

    total = acc[...]
    for step in range(1, depth):
        arrived(z_in.at[ahead(step), :, first], pza_r.at[ahead(step)])
        arrived(z_in.at[ahead(step), :, second], pzb_r.at[ahead(step)])
        total = total + z_in[ahead(step)].astype(f32)
    out[...] = total.astype(bf16)

    arrived(meta.at[0], fx_s.at[0])
    for s in range(depth):
        passed(s, meta.at[s], m_s)
        passed(s, tok.at[s], zt_s)
        passed(s, far_meta.at[s], fm_s)
        if cut_mid < width:
            passed(s, far_tok.at[s, :, rest], zf_s)

        @pl.when(s == z)
        def _():
            arrived(far_tok.at[s, :, wide], raw_s.at[s])

        @pl.when(s != z)
        def _():
            arrived(z_out.at[s, :, first], pza_s.at[s])
            arrived(z_out.at[s, :, second], pzb_s.at[s])
            if cut_mid > cut_in:
                arrived(far_tok.at[s, :, mid], raw_s.at[s])

        slab = x_buf.at[s, pl.ds(0, cap), near]
        for sem in (ya_s, xa_s, xb_s):
            arrived(slab, sem.at[s])
        arrived(y_pick.at[s, :, wide], yb_s.at[s])
        arrived(c_in.at[s], c_s.at[s])
        arrived(c_in.at[s], pc_s.at[s])
        arrived(x_out.at[s, :, first], pxa_s.at[s])
        arrived(y_out.at[s, pl.ds(0, cap), first], pya_s.at[s])
        arrived(y_out.at[s, :, second], pyb_s.at[s])
        arrived(x_out.at[s, pl.ds(0, rows), second], pxb_s.at[s])


CUTS = (1664, 2560, 1408)
PLAN = (
    ("ffn_down", (7, 8, 13, 12)),
    ("choose", (0, 3, 5, 7)),
    ("sum_x", (18, 12, 17, 13)),
    ("forward", (1, 3, 9, 8)),
    ("relay", (None, 1, 2, 5)),
    ("to_core", (3, 6, 12, 10)),
    ("sum_y", (17, 11, 16, 14)),
    ("sum_core", (16, 9, 14, 12)),
    ("comb_b", (18, 12, 16, 15)),
    ("comb_a", (18, 13, 17, 14)),
    ("ffn_up", (5, 7, 12, 10)),
    ("relay_far", (None, 4, 3, 7)),
    ("choose_far", (0, 4, 9, 7)),
)


def gathered_plan(tokens, expert_ids, gate_codes, w_gate, w_up, w_down, capacity, expert_count):
    rows, top = expert_ids.shape
    width = tokens.shape[1]
    w_gate, w_up = jnp.swapaxes(w_gate, 1, 2), jnp.swapaxes(w_up, 1, 2)
    part_width = w_gate.shape[1]
    depth = lax.axis_size("expert") // 2
    f32, bf16 = jnp.float32, jnp.bfloat16
    group = 2 * capacity
    vm, dma = pltpu.VMEM, pltpu.SemaphoreType.DMA
    one, two = dma((depth,)), dma((2, depth))
    return pl.pallas_call(
        functools.partial(fused, depth, expert_count, capacity, *CUTS, PLAN),
        out_shape=jax.ShapeDtypeStruct((rows, width), bf16),
        in_specs=[pl.BlockSpec(memory_space=pl.ANY)]
        + [pl.BlockSpec(memory_space=pltpu.VMEM)] * 2
        + [pl.BlockSpec(memory_space=pl.ANY)] * 3,
        out_specs=pl.BlockSpec(memory_space=pltpu.VMEM),
        scratch_shapes=[
            vm((depth, rows, width), bf16),
            vm((depth, rows, width), bf16),
            vm((depth, 2 * expert_count, rows), f32),
            vm((depth, 2 * expert_count, rows), f32),
            vm((depth, group, width), bf16),
            vm((depth, 4 * group, width), bf16),
            vm(w_gate.shape[1:], bf16),
            vm(w_up.shape[1:], bf16),
            vm(w_down.shape[1:], bf16),
            vm((4 * group, part_width), bf16),
            vm((depth, 4 * group, width), bf16),
            vm((depth, 2 * group, width), bf16),
            vm((depth, group, width), bf16),
            vm((depth, group, width), bf16),
            vm((depth, group, width), bf16),
            vm((depth, group, width), bf16),
            vm((depth, rows, width), bf16),
            vm((depth, rows, width), bf16),
            vm((rows, width), f32),
            dma((3,)),
        ]
        + [two, one] * 4
        + [dma((1,))]
        + [one] * 26,
        compiler_params=pltpu.CompilerParams(
            collective_id=0, has_side_effects=True, vmem_limit_bytes=63 << 20
        ),
    )(tokens, expert_ids.T, gate_codes.T, w_gate, w_up, w_down)


def slot_plan(tokens, expert_ids, gate_codes, w_gate, w_up, w_down):
    tok_rows, top_count = expert_ids.shape
    width = tokens.shape[1]
    expert_count = lax.axis_size("expert") * w_gate.shape[0]
    capacity = 3 * tok_rows * top_count // (2 * expert_count)
    slot_count = expert_count * capacity
    flat_ids = expert_ids.reshape(-1)
    onehot = (flat_ids[:, None] == jnp.arange(expert_count, dtype=jnp.int32)[None, :]).astype(
        jnp.int32
    )
    ranking = jnp.sum((jnp.cumsum(onehot, axis=0) - 1) * onehot, axis=1)
    target = flat_ids * capacity + ranking
    picker = (target[:, None] == jnp.arange(slot_count, dtype=jnp.int32)[None, :]).astype(
        jnp.bfloat16
    )
    selector = jnp.sum(picker.reshape(tok_rows, top_count, slot_count), axis=1)
    outgoing = jnp.einsum("ts,td->sd", selector, tokens, preferred_element_type=jnp.float32).astype(
        jnp.bfloat16
    )
    arrived = lax.all_to_all(outgoing, "expert", split_axis=0, concat_axis=0, tiled=True)
    gathered = lax.all_gather(arrived, "replica", axis=0, tiled=True)
    gate = jnp.dot(gathered, w_gate[0], preferred_element_type=jnp.float32)
    up = jnp.dot(gathered, w_up[0], preferred_element_type=jnp.float32)
    hidden = activate(gate, up).astype(jnp.bfloat16)
    summed = lax.psum_scatter(
        jnp.dot(hidden, w_down[0], preferred_element_type=jnp.float32).astype(jnp.bfloat16),
        "replica",
        scatter_dimension=0,
        tiled=True,
    )
    returned = lax.all_to_all(summed, "expert", split_axis=0, concat_axis=0, tiled=True)
    per_choice = jnp.dot(picker, returned, preferred_element_type=jnp.float32)
    gates = gate_codes.astype(jnp.float32) / 65536.0
    weighted = per_choice.reshape(tok_rows, top_count, width) * gates[:, :, None]
    return jnp.sum(weighted, axis=1).astype(jnp.bfloat16)


def on_device(tokens, expert_ids, gate_codes, w_gate, w_up, w_down):
    rows, top = expert_ids.shape
    expert_count = lax.axis_size("expert") * w_gate.shape[0]
    capacity = 3 * rows * top // (2 * expert_count)
    args = (tokens, expert_ids, gate_codes, w_gate, w_up, w_down)
    paired = w_gate.shape[0] == 1 and lax.axis_size("replica") == 2 * CORES
    if paired and 2 * capacity > rows:
        return gathered_plan(*args, capacity, expert_count)
    return slot_plan(*args)


def solution(mesh):
    return jax.shard_map(
        on_device,
        mesh=mesh,
        in_specs=(
            P(("expert", "replica"), None),
            P(("expert", "replica"), None),
            P(("expert", "replica"), None),
            P("expert", None, "replica"),
            P("expert", None, "replica"),
            P("expert", "replica", None),
        ),
        out_specs=P(("expert", "replica"), None),
        check_vma=False,
    )
```

```python
import functools

import jax
import jax.numpy as jnp
from jax import lax
from jax.experimental import pallas as pl
from jax.experimental.pallas import tpu as pltpu
from jax.sharding import PartitionSpec as P

MESH = pl.DeviceIdType.MESH
CORES = 2


def activate(gate, up):
    return gate * jax.nn.sigmoid(1.702 * gate) * (up + 1.0)


def spans(extent, step):
    return [(low, min(low + step, extent)) for low in range(0, extent, step)]


def fused(
    depth, experts, cap, in_parts, out_parts, plan,
    tokens, ids, codes, w_gate, w_up, w_down, out,
    tok, far_tok, meta, far_meta, y_pick, x_buf, wg, wu, wd, hid, part, c_in,
    x_out, x_in, y_out, y_in, z_out, z_in, mid_in, acc, far_acc, last_out, last_in,
    w_sem, m_s, m_r, fm_s, fm_r, fx_s,
    zt_s, zt_r, zf_s, zf_r, raw_s, raw_r, yp_s, yp_r, xa_s, xa_r, xb_s, xb_r, cc_s, cc_r,
    pc_s, pc_r, px_s, px_r, py_s, py_r, pz_s, pz_r, mi_r, last_s, last_r,
):
    rows, width = tokens.shape
    f32, bf16 = jnp.float32, jnp.bfloat16
    expert, replica = lax.axis_index("expert"), lax.axis_index("replica")
    z, y = expert // 2, expert % 2
    other = z * 2 + (1 - y)
    y_peer = {"expert": other}
    x_peer = {"replica": (replica + CORES) % (2 * CORES)}
    c_peer = {"replica": replica // CORES * CORES + (1 - replica % CORES)}
    group = 2 * cap
    own_slots, mine = pl.ds(0, cap), pl.ds(0, 2 * group)

    def z_peer(level):
        return {"expert": level * 2 + y}

    def ahead(step):
        return (z + step) % depth

    def send(src, dst, ssem, rsem, peer):
        pltpu.make_async_remote_copy(
            src_ref=src, dst_ref=dst, send_sem=ssem, recv_sem=rsem,
            device_id=peer, device_id_type=MESH,
        ).start()

    def arrived(dst, sem):
        pltpu.make_async_copy(dst, dst, sem).wait()

    def block_at(i):
        pairs = jnp.minimum(z, depth - 1 - z)
        inward = jnp.where(2 * z < depth, 1, -1)
        beside = jnp.where(i % 2 == 1, z + inward * ((i + 1) // 2), z - inward * (i // 2))
        beyond = jnp.where(2 * z < depth, i, depth - 1 - i)
        return jnp.where(i <= 2 * pairs, beside, beyond)

    def cols(parts, p):
        _, low, high = parts[p]
        return pl.ds(low, high - low)

    barrier = pltpu.get_barrier_semaphore()
    greeted = [y_peer, x_peer, c_peer] + [z_peer(ahead(step)) for step in range(1, depth)]
    for peer in greeted:
        pl.semaphore_signal(barrier, inc=1, device_id=peer, device_id_type=MESH)
    own_load = pltpu.make_async_copy(tokens, tok.at[z], w_sem.at[3])
    own_load.start()
    loads = [
        pltpu.make_async_copy(src.at[0], dst, w_sem.at[i])
        for i, (src, dst) in enumerate(((w_gate, wg), (w_up, wu), (w_down, wd)))
    ]
    for load in loads:
        load.start()

    label = lax.broadcasted_iota(jnp.int32, (experts, rows), 0)
    named = jnp.zeros((experts, rows), f32)
    weight = jnp.zeros((experts, rows), f32)
    for k in range(ids.shape[0]):
        same = label == ids[k : k + 1, :]
        named = named + jnp.where(same, 1.0, 0.0)
        weight = weight + jnp.where(same, codes[k : k + 1, :].astype(f32) / 65536.0, 0.0)
    upto = lax.broadcasted_iota(jnp.int32, (rows, rows), 0) <= lax.broadcasted_iota(
        jnp.int32, (rows, rows), 1
    )
    counts = jnp.dot(
        named.astype(bf16), jnp.where(upto, 1.0, 0.0).astype(bf16), preferred_element_type=f32
    )
    meta[z, pl.ds(0, experts), :] = jnp.where(named > 0, counts - 1.0, -1.0)
    meta[z, pl.ds(experts, experts), :] = weight

    pl.semaphore_wait(barrier, len(greeted))
    own_load.wait()

    def upward(s):
        return (s <= z) & (z < depth - 1)

    def downward(s):
        return (s >= z) & (z > 0)

    def pass_on(s, src, up_sem, down_sem, rsem):
        @pl.when(upward(s))
        def _():
            send(src, src, up_sem, rsem, z_peer(ahead(1)))

        @pl.when(downward(s))
        def _():
            send(src, src, down_sem, rsem, z_peer(ahead(depth - 1)))

    def passed(s, src, up_sem, down_sem):
        @pl.when(upward(s))
        def _():
            arrived(src, up_sem)

        @pl.when(downward(s))
        def _():
            arrived(src, down_sem)

    def pass_tok(p, s):
        pass_on(s, tok.at[s, :, cols(in_parts, p)], zt_s.at[p, 0, s], zt_s.at[p, 1, s], zt_r.at[p, s])

    def pass_far(p, s):
        pass_on(s, far_tok.at[s, :, cols(in_parts, p)], zf_s.at[p, 0, s], zf_s.at[p, 1, s], zf_r.at[p, s])

    def send_raw(p, s):
        c = cols(in_parts, p)
        send(tok.at[s, :, c], far_tok.at[s, :, c], raw_s.at[p, s], raw_r.at[p, s], x_peer)

    send(meta.at[z], far_meta.at[z], fx_s.at[0], fm_r.at[z], x_peer)
    pass_on(z, meta.at[z], m_s.at[0, z], m_s.at[1, z], m_r.at[z])
    for p in range(len(in_parts)):
        pass_tok(p, z)
    for p, (kind, _, _) in enumerate(in_parts):
        if kind != "A":
            send_raw(p, z)

    def row_of(table, which):
        sub = lax.broadcasted_iota(jnp.int32, table.shape, 0)
        return jnp.sum(jnp.where(sub == which, table, 0.0), axis=0, keepdims=True)

    def slots(table, which):
        slot = lax.broadcasted_iota(jnp.int32, (cap, rows), 0).astype(f32)
        return slot == row_of(table, which)

    def picker(table):
        return jnp.concatenate(
            [jnp.where(slots(table, e), 1.0, 0.0) for e in (expert, other)], axis=0
        ).astype(bf16)

    def spreader(table):
        high, low = [], []
        for e in (expert, other):
            share = row_of(table, e + experts)
            coarse = share.astype(bf16).astype(f32)
            here = slots(table, e)
            high.append(jnp.where(here, coarse, 0.0))
            low.append(jnp.where(here, share - coarse, 0.0))
        return jnp.concatenate(high + low, axis=0).astype(bf16)

    def spread(table, own, far):
        stacked = jnp.concatenate([own, far, own, far], axis=0)
        return lax.dot_general(
            spreader(table), stacked, (((0,), (0,)), ((), ())), preferred_element_type=f32
        )

    def greet(p, i):
        s = block_at(i)

        @pl.when(i > 0)
        def _():
            arrived(meta.at[s], m_r.at[s])
            pass_on(s, meta.at[s], m_s.at[0, s], m_s.at[1, s], m_r.at[s])

        arrived(far_meta.at[s], fm_r.at[s])
        pass_on(s, far_meta.at[s], fm_s.at[0, s], fm_s.at[1, s], fm_r.at[s])

    def relay(p, i):
        s = block_at(i)
        kind, c = in_parts[p][0], cols(in_parts, p)
        arrived(tok.at[s, :, c], zt_r.at[p, s])
        pass_tok(p, s)
        if kind == "C":
            arrived(far_tok.at[s, :, c], zf_r.at[p, s])
            pass_far(p, s)
        if kind == "B":
            send_raw(p, s)

    def choose(p, i):
        s = block_at(i)
        kind, c = in_parts[p][0], cols(in_parts, p)

        def pick(table, block, low):
            chosen = jnp.dot(picker(table[s]), block[s, :, c], preferred_element_type=f32).astype(bf16)
            x_buf[s, pl.ds(low, cap), c] = chosen[:cap]
            y_pick[s, pl.ds(low, cap), c] = chosen[cap:]

        if kind == "A":
            pick(meta, tok, 0)
            send(y_pick.at[s, own_slots, c], x_buf.at[s, pl.ds(group, cap), c],
                 yp_s.at[p, s], yp_r.at[p, s], y_peer)
            send(x_buf.at[s, own_slots, c], x_buf.at[s, pl.ds(cap, cap), c],
                 xa_s.at[p, s], xa_r.at[p, s], x_peer)
            return

        @pl.when((i == 0) | (kind == "B"))
        def _():
            arrived(far_tok.at[s, :, c], raw_r.at[p, s])
            if kind == "C":
                pass_far(p, s)

        pick(meta, tok, 0)
        pick(far_meta, far_tok, cap)
        send(y_pick.at[s, :, c], x_buf.at[s, pl.ds(group, group), c],
             yp_s.at[p, s], yp_r.at[p, s], y_peer)

    def forward(p, i):
        s = block_at(i)
        c = cols(in_parts, p)
        here = x_buf.at[s, pl.ds(group, cap), c]
        arrived(here, yp_r.at[p, s])
        send(here, x_buf.at[s, pl.ds(group + cap, cap), c], xb_s.at[p, s], xb_r.at[p, s], x_peer)

    def to_core(p, i):
        s = block_at(i)
        kind, c = in_parts[p][0], cols(in_parts, p)
        if kind == "A":
            arrived(x_buf.at[s, pl.ds(cap, cap), c], xa_r.at[p, s])
            arrived(x_buf.at[s, pl.ds(group + cap, cap), c], xb_r.at[p, s])
        else:
            arrived(x_buf.at[s, pl.ds(group, group), c], yp_r.at[p, s])
        send(x_buf.at[s, mine, c], x_buf.at[s, pl.ds(2 * group, 2 * group), c],
             cc_s.at[p, s], cc_r.at[p, s], c_peer)

    starts = dict(plan)
    first_up = min((t, i) for i, t in enumerate(starts["up", 0]))[1]
    thirds = spans(wg.shape[0], -(-wg.shape[0] // (3 * 128)) * 128)

    def up(p, i):
        s = block_at(i)
        if p == 0:
            for q in range(len(in_parts)):
                arrived(x_buf.at[s, mine, cols(in_parts, q)], cc_r.at[q, s])

            @pl.when(i == first_up)
            def _():
                for load in loads:
                    load.wait()

        across = (((1,), (1,)), ((), ()))
        low, high = thirds[p]
        block = x_buf[s]
        gate = lax.dot_general(block, wg[low:high, :], across, preferred_element_type=f32)
        more = lax.dot_general(block, wu[low:high, :], across, preferred_element_type=f32)
        hid[:, low:high] = activate(gate, more).astype(bf16)

    def down(p, i):
        s = block_at(i)
        _, start, stop = out_parts[p]
        for low, high in spans(stop - start, 512):
            here = slice(start + low, start + high)
            part[s, :, here] = jnp.dot(
                hid[...], wd[:, here], preferred_element_type=f32
            ).astype(bf16)
        c = cols(out_parts, p)
        send(part.at[s, pl.ds(2 * group, 2 * group), c], c_in.at[s, :, c],
             pc_s.at[p, s], pc_r.at[p, s], c_peer)

    def pair(s, low, count, c):
        return part[s, pl.ds(low, count), c].astype(f32) + c_in[s, pl.ds(low, count), c].astype(f32)

    def core(p, j):
        s = block_at(j)
        kind, c = out_parts[p][0], cols(out_parts, p)
        arrived(c_in.at[s, :, c], pc_r.at[p, s])
        if kind == "A":
            for n in range(2):
                x_out[s, pl.ds(n * cap, cap), c] = pair(s, cap + n * group, cap, c).astype(bf16)
            send(x_out.at[s, :, c], x_in.at[s, :, c], px_s.at[p, s], px_r.at[p, s], x_peer)
        else:
            y_out[s, :, c] = pair(s, group, group, c).astype(bf16)
            send(y_out.at[s, :, c], y_in.at[s, :, c], py_s.at[p, s], py_r.at[p, s], y_peer)

    def detour(source, owner):
        return ((source == 0) & (owner > 1)) | ((source == depth - 1) & (owner < depth - 2))

    def joins(s):
        return ((z == 1) & (s > 1)) | ((z == depth - 2) & (s < depth - 2))

    def z_rows(p):
        return pl.ds(0, 2 * rows if out_parts[p][0] == "C" else rows)

    def z_send(p, s, ready):
        c, r = cols(out_parts, p), z_rows(p)

        @pl.when(ready & detour(z, s))
        def _():
            send(z_out.at[s, r, c], mid_in.at[s, r, c], pz_s.at[p, s], mi_r.at[p, s],
                 z_peer(jnp.where(z == 0, 1, depth - 2)))

        @pl.when(ready & jnp.logical_not(detour(z, s)))
        def _():
            send(z_out.at[s, r, c], z_in.at[z, r, c], pz_s.at[p, s], pz_r.at[p, z], z_peer(s))

    def deliver(p, s, total, far=None):
        c = cols(out_parts, p)

        @pl.when(s == z)
        def _():
            acc[:, c] = total
            if far is not None:
                far_acc[:, c] = far

        @pl.when(s != z)
        def _():
            z_out[s, pl.ds(0, rows), c] = total.astype(bf16)
            if far is not None:
                z_out[s, pl.ds(rows, rows), c] = far.astype(bf16)

        z_send(p, s, (s != z) & jnp.logical_not(joins(s)))

    def far_mix(p, s):
        c = cols(out_parts, p)
        return spread(far_meta[s], pair(s, cap, cap, c).astype(bf16), y_in[s, pl.ds(cap, cap), c])

    def own_mix(p, s):
        c = cols(out_parts, p)
        return spread(meta[s], pair(s, 0, cap, c).astype(bf16), y_in[s, own_slots, c])

    def gather(p, j):
        s = block_at(j)
        kind, c = out_parts[p][0], cols(out_parts, p)
        if kind == "A":
            arrived(x_in.at[s, :, c], px_r.at[p, s])
            y_out[s, own_slots, c] = (
                pair(s, group, cap, c) + x_in[s, pl.ds(cap, cap), c].astype(f32)
            ).astype(bf16)
            send(y_out.at[s, own_slots, c], y_in.at[s, own_slots, c],
                 py_s.at[p, s], py_r.at[p, s], y_peer)
            return
        arrived(y_in.at[s, :, c], py_r.at[p, s])
        if kind == "B":
            x_out[s, pl.ds(0, rows), c] = far_mix(p, s).astype(bf16)
            send(x_out.at[s, pl.ds(0, rows), c], x_in.at[s, pl.ds(0, rows), c],
                 px_s.at[p, s], px_r.at[p, s], x_peer)
        else:
            deliver(p, s, own_mix(p, s), far_mix(p, s))

    def comb(p, j):
        s = block_at(j)
        kind, c = out_parts[p][0], cols(out_parts, p)
        if kind == "A":
            arrived(y_in.at[s, own_slots, c], py_r.at[p, s])
            own = (pair(s, 0, cap, c) + x_in[s, own_slots, c].astype(f32)).astype(bf16)
            deliver(p, s, spread(meta[s], own, y_in[s, own_slots, c]))
        else:
            arrived(x_in.at[s, pl.ds(0, rows), c], px_r.at[p, s])
            deliver(p, s, own_mix(p, s) + x_in[s, pl.ds(0, rows), c].astype(f32))

    def chain(p, j):
        s = block_at(j)
        c, r = cols(out_parts, p), z_rows(p)

        @pl.when(joins(s))
        def _():
            arrived(mid_in.at[s, r, c], mi_r.at[p, s])
            z_out[s, r, c] = (z_out[s, r, c].astype(f32) + mid_in[s, r, c].astype(f32)).astype(bf16)

        z_send(p, s, joins(s))

    table = {
        "meta": greet, "relay": relay, "choose": choose, "forward": forward, "to_core": to_core,
        "up": up, "down": down, "core": core, "sum": gather, "comb": comb, "chain": chain,
    }

    order = sorted((t, k, key, i) for k, (key, at) in enumerate(plan) for i, t in enumerate(at) if t is not None)
    for _, _, (name, p), i in order:
        table[name](p, i)

    def collect(p):
        kind, c = out_parts[p][0], cols(out_parts, p)
        for step in range(1, depth):
            q = ahead(step)

            @pl.when(jnp.logical_not(detour(q, z)))
            def _():
                arrived(z_in.at[q, z_rows(p), c], pz_r.at[p, q])
                acc[:, c] = acc[:, c] + z_in[q, pl.ds(0, rows), c].astype(f32)
                if kind == "C":
                    far_acc[:, c] = far_acc[:, c] + z_in[q, pl.ds(rows, rows), c].astype(f32)

    crossing = [p for p, (kind, _, _) in enumerate(out_parts) if kind == "C"]
    for p in crossing:
        c = cols(out_parts, p)
        collect(p)
        last_out[:, c] = far_acc[:, c].astype(bf16)
        send(last_out.at[:, c], last_in.at[:, c], last_s.at[p], last_r.at[p], x_peer)
    for p in range(len(out_parts)):
        if p not in crossing:
            c = cols(out_parts, p)
            collect(p)
            out[:, c] = acc[:, c].astype(bf16)
    for p in crossing:
        c = cols(out_parts, p)
        arrived(last_in.at[:, c], last_r.at[p])
        out[:, c] = (acc[:, c] + last_in[:, c].astype(f32)).astype(bf16)

    arrived(meta.at[0], fx_s.at[0])
    for p in crossing:
        arrived(last_out.at[:, cols(out_parts, p)], last_s.at[p])

    def settle(s, carry):
        passed(s, meta.at[s], m_s.at[0, s], m_s.at[1, s])
        passed(s, far_meta.at[s], fm_s.at[0, s], fm_s.at[1, s])
        for p, (kind, _, _) in enumerate(in_parts):
            c = cols(in_parts, p)
            passed(s, tok.at[s, :, c], zt_s.at[p, 0, s], zt_s.at[p, 1, s])
            if kind == "C":
                passed(s, far_tok.at[s, :, c], zf_s.at[p, 0, s], zf_s.at[p, 1, s])
            if kind != "A":
                @pl.when((s == z) | (kind == "B"))
                def _():
                    arrived(far_tok.at[s, :, c], raw_s.at[p, s])

                arrived(y_pick.at[s, :, c], yp_s.at[p, s])
            else:
                slab = x_buf.at[s, own_slots, c]
                for sem in (yp_s, xa_s, xb_s):
                    arrived(slab, sem.at[p, s])
            arrived(x_buf.at[s, mine, c], cc_s.at[p, s])
        for p, (kind, _, _) in enumerate(out_parts):
            c = cols(out_parts, p)
            arrived(c_in.at[s, :, c], pc_s.at[p, s])
            if kind == "A":
                arrived(x_out.at[s, :, c], px_s.at[p, s])
                arrived(y_out.at[s, own_slots, c], py_s.at[p, s])
            else:
                arrived(y_out.at[s, :, c], py_s.at[p, s])
                if kind == "B":
                    arrived(x_out.at[s, pl.ds(0, rows), c], px_s.at[p, s])

            @pl.when(s != z)
            def _():
                arrived(z_out.at[s, z_rows(p), c], pz_s.at[p, s])
        return carry

    lax.fori_loop(0, depth, settle, 0)


IN_PARTS = (("A", 0), ("A", 1024), ("C", 2048))
OUT_PARTS = (("A", 0), ("A", 1152), ("C", 1792), ("C", 2304))
PLAN = (
    (("sum", 1), (28, 33, 27, 26)),
    (("meta", 0), (0, 1, 2, 10)),
    (("relay", 0), (None, 2, 5, 9)),
    (("to_core", 0), (2, 8, 14, 18)),
    (("core", 2), (17, 16, 19, 23)),
    (("comb", 0), (33, 32, 29, 31)),
    (("relay", 1), (None, 1, 5, 11)),
    (("choose", 0), (0, 2, 6, 10)),
    (("choose", 1), (0, 1, 5, 13)),
    (("down", 3), (7, 13, 18, 22)),
    (("forward", 0), (0, 4, 11, 16)),
    (("core", 1), (11, 27, 19, 25)),
    (("chain", 0), (None, 32, 34, 33)),
    (("up", 2), (6, 12, 17, 21)),
    (("core", 0), (26, 17, 20, 25)),
    (("to_core", 1), (2, 7, 13, 17)),
    (("sum", 2), (24, 19, 21, 25)),
    (("chain", 2), (None, 25, 34, 29)),
    (("sum", 0), (31, 30, 25, 29)),
    (("choose", 2), (0, 3, 7, 14)),
    (("down", 2), (6, 14, 17, 21)),
    (("comb", 1), (30, 33, 31, 28)),
    (("core", 3), (10, 14, 20, 24)),
    (("up", 0), (3, 10, 16, 19)),
    (("chain", 3), (None, 27, 24, 30)),
    (("down", 0), (9, 14, 18, 21)),
    (("up", 1), (3, 11, 16, 19)),
    (("to_core", 2), (1, 6, 12, 16)),
    (("down", 1), (8, 15, 17, 23)),
    (("relay", 2), (None, 2, 6, 13)),
    (("sum", 3), (30, 17, 23, 25)),
    (("forward", 1), (0, 2, 8, 14)),
    (("chain", 1), (None, 34, 33, 30)),
)


def gathered_plan(tokens, expert_ids, gate_codes, w_gate, w_up, w_down, capacity, expert_count):
    rows, top = expert_ids.shape
    width = tokens.shape[1]
    w_gate, w_up = jnp.swapaxes(w_gate, 1, 2), jnp.swapaxes(w_up, 1, 2)
    part_width = w_gate.shape[1]
    depth = lax.axis_size("expert") // 2
    f32, bf16 = jnp.float32, jnp.bfloat16
    group = 2 * capacity
    vm, dma = pltpu.VMEM, pltpu.SemaphoreType.DMA

    def bounds(parts):
        lows = [low for _, low in parts]
        return [(kind, low, high) for (kind, low), high in zip(parts, lows[1:] + [width])]

    in_parts, out_parts = bounds(IN_PARTS), bounds(OUT_PARTS)
    ins, outs = len(in_parts), len(out_parts)
    two, one = dma((ins, 2, depth)), dma((ins, depth))
    block = vm((depth, group, width), bf16)
    pair = vm((depth, 2 * rows, width), bf16)
    return pl.pallas_call(
        functools.partial(fused, depth, expert_count, capacity, in_parts, out_parts, PLAN),
        out_shape=jax.ShapeDtypeStruct((rows, width), bf16),
        in_specs=[pl.BlockSpec(memory_space=pl.ANY)]
        + [pl.BlockSpec(memory_space=pltpu.VMEM)] * 2
        + [pl.BlockSpec(memory_space=pl.ANY)] * 3,
        out_specs=pl.BlockSpec(memory_space=pltpu.VMEM),
        scratch_shapes=[
            vm((depth, rows, width), bf16),
            vm((depth, rows, width), bf16),
            vm((depth, 2 * expert_count, rows), f32),
            vm((depth, 2 * expert_count, rows), f32),
            block,
            vm((depth, 4 * group, width), bf16),
            vm(w_gate.shape[1:], bf16),
            vm(w_up.shape[1:], bf16),
            vm(w_down.shape[1:], bf16),
            vm((4 * group, part_width), bf16),
            vm((depth, 4 * group, width), bf16),
            vm((depth, 2 * group, width), bf16),
            block,
            block,
            block,
            block,
            pair,
            pair,
            pair,
            vm((rows, width), f32),
            vm((rows, width), f32),
            vm((rows, width), bf16),
            vm((rows, width), bf16),
            dma((4,)),
            dma((2, depth)),
            dma((depth,)),
            dma((2, depth)),
            dma((depth,)),
            dma((1,)),
            two,
            one,
            two,
        ]
        + [one] * 11
        + [dma((outs, depth))] * 9
        + [dma((outs,))] * 2,
        compiler_params=pltpu.CompilerParams(
            collective_id=0, has_side_effects=True, vmem_limit_bytes=63 << 20
        ),
    )(tokens, expert_ids.T, gate_codes.T, w_gate, w_up, w_down)


def slot_plan(tokens, expert_ids, gate_codes, w_gate, w_up, w_down):
    tok_rows, top_count = expert_ids.shape
    width = tokens.shape[1]
    expert_count = lax.axis_size("expert") * w_gate.shape[0]
    capacity = 3 * tok_rows * top_count // (2 * expert_count)
    slot_count = expert_count * capacity
    flat_ids = expert_ids.reshape(-1)
    onehot = (flat_ids[:, None] == jnp.arange(expert_count, dtype=jnp.int32)[None, :]).astype(
        jnp.int32
    )
    ranking = jnp.sum((jnp.cumsum(onehot, axis=0) - 1) * onehot, axis=1)
    target = flat_ids * capacity + ranking
    picker = (target[:, None] == jnp.arange(slot_count, dtype=jnp.int32)[None, :]).astype(
        jnp.bfloat16
    )
    selector = jnp.sum(picker.reshape(tok_rows, top_count, slot_count), axis=1)
    outgoing = jnp.einsum("ts,td->sd", selector, tokens, preferred_element_type=jnp.float32).astype(
        jnp.bfloat16
    )
    arrived = lax.all_to_all(outgoing, "expert", split_axis=0, concat_axis=0, tiled=True)
    gathered = lax.all_gather(arrived, "replica", axis=0, tiled=True)
    gate = jnp.dot(gathered, w_gate[0], preferred_element_type=jnp.float32)
    up = jnp.dot(gathered, w_up[0], preferred_element_type=jnp.float32)
    hidden = activate(gate, up).astype(jnp.bfloat16)
    summed = lax.psum_scatter(
        jnp.dot(hidden, w_down[0], preferred_element_type=jnp.float32).astype(jnp.bfloat16),
        "replica",
        scatter_dimension=0,
        tiled=True,
    )
    returned = lax.all_to_all(summed, "expert", split_axis=0, concat_axis=0, tiled=True)
    per_choice = jnp.dot(picker, returned, preferred_element_type=jnp.float32)
    gates = gate_codes.astype(jnp.float32) / 65536.0
    weighted = per_choice.reshape(tok_rows, top_count, width) * gates[:, :, None]
    return jnp.sum(weighted, axis=1).astype(jnp.bfloat16)


def on_device(tokens, expert_ids, gate_codes, w_gate, w_up, w_down):
    rows, top = expert_ids.shape
    expert_count = lax.axis_size("expert") * w_gate.shape[0]
    capacity = 3 * rows * top // (2 * expert_count)
    args = (tokens, expert_ids, gate_codes, w_gate, w_up, w_down)
    paired = w_gate.shape[0] == 1 and lax.axis_size("replica") == 2 * CORES
    if paired and 2 * capacity > rows:
        return gathered_plan(*args, capacity, expert_count)
    return slot_plan(*args)


def solution(mesh):
    return jax.shard_map(
        on_device,
        mesh=mesh,
        in_specs=(
            P(("expert", "replica"), None),
            P(("expert", "replica"), None),
            P(("expert", "replica"), None),
            P("expert", None, "replica"),
            P("expert", None, "replica"),
            P("expert", "replica", None),
        ),
        out_specs=P(("expert", "replica"), None),
        check_vma=False,
    )
```

```python
import functools

import jax
import jax.numpy as jnp
from jax import lax
from jax.experimental import pallas as pl
from jax.experimental.pallas import tpu as pltpu
from jax.sharding import PartitionSpec as P

MESH = pl.DeviceIdType.MESH
CORES = 2


def activate(gate, up):
    return gate * jax.nn.sigmoid(1.702 * gate) * (up + 1.0)


def spans(extent, step):
    return [(low, min(low + step, extent)) for low in range(0, extent, step)]


def fused(
    depth, experts, cap, in_parts, out_parts, plan,
    tokens, ids_in, codes_in, w_gate, w_up, w_down, out,
    ids, codes, done, tok, far_tok, meta, far_meta, y_pick, x_buf, wg, wu, wd, hid, part, c_in,
    x_out, x_in, y_out, y_in, z_out, z_in, mid_in, acc, far_acc, last_out, last_in,
    w_sem, out_sem, m_s, m_r, fm_s, fm_r, fx_s,
    zt_s, zt_r, zf_s, zf_r, raw_s, raw_r, yp_s, yp_r, xa_s, xa_r, xb_s, xb_r, cc_s, cc_r,
    pc_s, pc_r, px_s, px_r, py_s, py_r, pz_s, pz_r, mi_r, last_s, last_r,
):
    rows, width = tokens.shape
    f32, bf16 = jnp.float32, jnp.bfloat16
    expert, replica = lax.axis_index("expert"), lax.axis_index("replica")
    z, y = expert // 2, expert % 2
    other = z * 2 + (1 - y)
    y_peer = {"expert": other}
    x_peer = {"replica": (replica + CORES) % (2 * CORES)}
    c_peer = {"replica": replica // CORES * CORES + (1 - replica % CORES)}
    group = 2 * cap
    own_slots, mine = pl.ds(0, cap), pl.ds(0, 2 * group)

    def z_peer(level):
        return {"expert": level * 2 + y}

    def ahead(step):
        return (z + step) % depth

    def send(src, dst, ssem, rsem, peer):
        pltpu.make_async_remote_copy(
            src_ref=src, dst_ref=dst, send_sem=ssem, recv_sem=rsem,
            device_id=peer, device_id_type=MESH,
        ).start()

    def arrived(dst, sem):
        pltpu.make_async_copy(dst, dst, sem).wait()

    def block_at(i):
        pairs = jnp.minimum(z, depth - 1 - z)
        inward = jnp.where(2 * z < depth, 1, -1)
        beside = jnp.where(i % 2 == 1, z + inward * ((i + 1) // 2), z - inward * (i // 2))
        beyond = jnp.where(2 * z < depth, i, depth - 1 - i)
        return jnp.where(i <= 2 * pairs, beside, beyond)

    def cols(parts, p):
        _, low, high = parts[p]
        return pl.ds(low, high - low)

    barrier = pltpu.get_barrier_semaphore()
    for peer in (y_peer, x_peer, c_peer):
        pl.semaphore_signal(barrier, inc=1, device_id=peer, device_id_type=MESH)
    for inside, step in ((z < depth - 1, 1), (z > 0, depth - 1)):
        @pl.when(inside)
        def _():
            pl.semaphore_signal(
                barrier, inc=1, device_id=z_peer(ahead(step)), device_id_type=MESH
            )

    neighbours = 3 + jnp.where(z < depth - 1, 1, 0) + jnp.where(z > 0, 1, 0)
    own_load = pltpu.make_async_copy(tokens, tok.at[z], w_sem.at[3])
    id_load = pltpu.make_async_copy(ids_in, ids, w_sem.at[4])
    code_load = pltpu.make_async_copy(codes_in, codes, w_sem.at[5])
    for load in (own_load, id_load, code_load):
        load.start()
    loads = [
        pltpu.make_async_copy(src.at[0], dst, w_sem.at[i])
        for i, (src, dst) in enumerate(((w_gate, wg), (w_up, wu), (w_down, wd)))
    ]
    for load in loads:
        load.start()

    pl.semaphore_wait(barrier, neighbours)
    own_load.wait()

    def upward(s):
        return (s <= z) & (z < depth - 1)

    def downward(s):
        return (s >= z) & (z > 0)

    def pass_on(s, src, up_sem, down_sem, rsem):
        @pl.when(upward(s))
        def _():
            send(src, src, up_sem, rsem, z_peer(ahead(1)))

        @pl.when(downward(s))
        def _():
            send(src, src, down_sem, rsem, z_peer(ahead(depth - 1)))

    def passed(s, src, up_sem, down_sem):
        @pl.when(upward(s))
        def _():
            arrived(src, up_sem)

        @pl.when(downward(s))
        def _():
            arrived(src, down_sem)

    def pass_tok(p, s):
        pass_on(s, tok.at[s, :, cols(in_parts, p)], zt_s.at[p, 0, s], zt_s.at[p, 1, s], zt_r.at[p, s])

    def pass_far(p, s):
        pass_on(s, far_tok.at[s, :, cols(in_parts, p)], zf_s.at[p, 0, s], zf_s.at[p, 1, s], zf_r.at[p, s])

    def send_raw(p, s):
        c = cols(in_parts, p)
        send(tok.at[s, :, c], far_tok.at[s, :, c], raw_s.at[p, s], raw_r.at[p, s], x_peer)

    pass_tok(0, z)
    id_load.wait()
    code_load.wait()
    label = lax.broadcasted_iota(jnp.int32, (experts, rows), 0)
    named = jnp.zeros((experts, rows), f32)
    weight = jnp.zeros((experts, rows), f32)
    for k in range(ids.shape[0]):
        same = label == ids[k : k + 1, :]
        named = named + jnp.where(same, 1.0, 0.0)
        weight = weight + jnp.where(same, codes[k : k + 1, :].astype(f32) / 65536.0, 0.0)
    upto = lax.broadcasted_iota(jnp.int32, (rows, rows), 0) <= lax.broadcasted_iota(
        jnp.int32, (rows, rows), 1
    )
    counts = jnp.dot(
        named.astype(bf16), jnp.where(upto, 1.0, 0.0).astype(bf16), preferred_element_type=f32
    )
    meta[z, pl.ds(0, experts), :] = jnp.where(named > 0, counts - 1.0, -1.0)
    meta[z, pl.ds(experts, experts), :] = weight
    send(meta.at[z], far_meta.at[z], fx_s.at[0], fm_r.at[z], x_peer)
    pass_on(z, meta.at[z], m_s.at[0, z], m_s.at[1, z], m_r.at[z])
    for p in range(1, len(in_parts)):
        pass_tok(p, z)
    for p, (kind, _, _) in enumerate(in_parts):
        if kind != "A":
            send_raw(p, z)

    def row_of(table, which):
        sub = lax.broadcasted_iota(jnp.int32, table.shape, 0)
        return jnp.sum(jnp.where(sub == which, table, 0.0), axis=0, keepdims=True)

    def slots(table, which):
        slot = lax.broadcasted_iota(jnp.int32, (cap, rows), 0).astype(f32)
        return slot == row_of(table, which)

    def picker(table):
        return jnp.concatenate(
            [jnp.where(slots(table, e), 1.0, 0.0) for e in (expert, other)], axis=0
        ).astype(bf16)

    def spreader(table):
        high, low = [], []
        for e in (expert, other):
            share = row_of(table, e + experts)
            coarse = share.astype(bf16).astype(f32)
            here = slots(table, e)
            high.append(jnp.where(here, coarse, 0.0))
            low.append(jnp.where(here, share - coarse, 0.0))
        return jnp.concatenate(high + low, axis=0).astype(bf16)

    def spread(table, own, far):
        stacked = jnp.concatenate([own, far, own, far], axis=0)
        return lax.dot_general(
            spreader(table), stacked, (((0,), (0,)), ((), ())), preferred_element_type=f32
        )

    def greet(p, i):
        s = block_at(i)

        @pl.when(i > 0)
        def _():
            arrived(meta.at[s], m_r.at[s])
            pass_on(s, meta.at[s], m_s.at[0, s], m_s.at[1, s], m_r.at[s])

        arrived(far_meta.at[s], fm_r.at[s])
        pass_on(s, far_meta.at[s], fm_s.at[0, s], fm_s.at[1, s], fm_r.at[s])

    def relay(p, i):
        s = block_at(i)
        kind, c = in_parts[p][0], cols(in_parts, p)
        arrived(tok.at[s, :, c], zt_r.at[p, s])
        pass_tok(p, s)
        if kind == "C":
            arrived(far_tok.at[s, :, c], zf_r.at[p, s])
            pass_far(p, s)
        if kind == "B":
            send_raw(p, s)

    def choose(p, i):
        s = block_at(i)
        kind, c = in_parts[p][0], cols(in_parts, p)

        def pick(table, block, low):
            chosen = jnp.dot(picker(table[s]), block[s, :, c], preferred_element_type=f32).astype(bf16)
            x_buf[s, pl.ds(low, cap), c] = chosen[:cap]
            y_pick[s, pl.ds(low, cap), c] = chosen[cap:]

        if kind == "A":
            pick(meta, tok, 0)
            send(y_pick.at[s, own_slots, c], x_buf.at[s, pl.ds(group, cap), c],
                 yp_s.at[p, s], yp_r.at[p, s], y_peer)
            send(x_buf.at[s, own_slots, c], x_buf.at[s, pl.ds(cap, cap), c],
                 xa_s.at[p, s], xa_r.at[p, s], x_peer)
            return

        @pl.when((i == 0) | (kind == "B"))
        def _():
            arrived(far_tok.at[s, :, c], raw_r.at[p, s])
            if kind == "C":
                pass_far(p, s)

        pick(meta, tok, 0)
        pick(far_meta, far_tok, cap)
        send(y_pick.at[s, :, c], x_buf.at[s, pl.ds(group, group), c],
             yp_s.at[p, s], yp_r.at[p, s], y_peer)

    def forward(p, i):
        s = block_at(i)
        c = cols(in_parts, p)
        here = x_buf.at[s, pl.ds(group, cap), c]
        arrived(here, yp_r.at[p, s])
        send(here, x_buf.at[s, pl.ds(group + cap, cap), c], xb_s.at[p, s], xb_r.at[p, s], x_peer)

    def to_core(p, i):
        s = block_at(i)
        kind, c = in_parts[p][0], cols(in_parts, p)
        if kind == "A":
            arrived(x_buf.at[s, pl.ds(cap, cap), c], xa_r.at[p, s])
            arrived(x_buf.at[s, pl.ds(group + cap, cap), c], xb_r.at[p, s])
        else:
            arrived(x_buf.at[s, pl.ds(group, group), c], yp_r.at[p, s])
        send(x_buf.at[s, mine, c], x_buf.at[s, pl.ds(2 * group, 2 * group), c],
             cc_s.at[p, s], cc_r.at[p, s], c_peer)

    first_up = next(i for name, _, i in plan if name == "up")
    ups = sum(1 for name, _, i in plan if name == "up" and i == first_up)
    pieces = spans(wg.shape[0], 256)

    def up(p, i):
        s = block_at(i)
        if p == 0:
            for q in range(len(in_parts)):
                arrived(x_buf.at[s, mine, cols(in_parts, q)], cc_r.at[q, s])

            @pl.when(i == first_up)
            def _():
                for load in loads:
                    load.wait()

        across = (((1,), (1,)), ((), ()))
        for low, high in pieces if ups == 1 else pieces[p::ups]:
            block = x_buf[s]
            gate = lax.dot_general(block, wg[low:high, :], across, preferred_element_type=f32)
            more = lax.dot_general(block, wu[low:high, :], across, preferred_element_type=f32)
            hid[:, low:high] = activate(gate, more).astype(bf16)

    def down(p, i):
        s = block_at(i)
        _, start, stop = out_parts[p]
        for low, high in spans(stop - start, 512):
            here = slice(start + low, start + high)
            part[s, :, here] = jnp.dot(
                hid[...], wd[:, here], preferred_element_type=f32
            ).astype(bf16)
        c = cols(out_parts, p)
        send(part.at[s, pl.ds(2 * group, 2 * group), c], c_in.at[s, :, c],
             pc_s.at[p, s], pc_r.at[p, s], c_peer)

    def pair(s, low, count, c):
        return part[s, pl.ds(low, count), c].astype(f32) + c_in[s, pl.ds(low, count), c].astype(f32)

    def core(p, j):
        s = block_at(j)
        kind, c = out_parts[p][0], cols(out_parts, p)
        arrived(c_in.at[s, :, c], pc_r.at[p, s])
        if kind == "A":
            for n in range(2):
                x_out[s, pl.ds(n * cap, cap), c] = pair(s, cap + n * group, cap, c).astype(bf16)
            send(x_out.at[s, :, c], x_in.at[s, :, c], px_s.at[p, s], px_r.at[p, s], x_peer)
        else:
            y_out[s, :, c] = pair(s, group, group, c).astype(bf16)
            send(y_out.at[s, :, c], y_in.at[s, :, c], py_s.at[p, s], py_r.at[p, s], y_peer)

    def detour(source, owner):
        return ((source == 0) & (owner > 1)) | ((source == depth - 1) & (owner < depth - 2))

    def joins(s):
        return ((z == 1) & (s > 1)) | ((z == depth - 2) & (s < depth - 2))

    def z_rows(p):
        return pl.ds(0, 2 * rows if out_parts[p][0] == "C" else rows)

    def z_send(p, s, ready):
        c, r = cols(out_parts, p), z_rows(p)

        @pl.when(ready & detour(z, s))
        def _():
            send(z_out.at[s, r, c], mid_in.at[s, r, c], pz_s.at[p, s], mi_r.at[p, s],
                 z_peer(jnp.where(z == 0, 1, depth - 2)))

        @pl.when(ready & jnp.logical_not(detour(z, s)))
        def _():
            send(z_out.at[s, r, c], z_in.at[z, r, c], pz_s.at[p, s], pz_r.at[p, z], z_peer(s))

    def deliver(p, s, total, far=None):
        c = cols(out_parts, p)

        @pl.when(s == z)
        def _():
            acc[:, c] = total
            if far is not None:
                far_acc[:, c] = far

        @pl.when(s != z)
        def _():
            z_out[s, pl.ds(0, rows), c] = total.astype(bf16)
            if far is not None:
                z_out[s, pl.ds(rows, rows), c] = far.astype(bf16)

        z_send(p, s, (s != z) & jnp.logical_not(joins(s)))

    def far_mix(p, s):
        c = cols(out_parts, p)
        return spread(far_meta[s], pair(s, cap, cap, c).astype(bf16), y_in[s, pl.ds(cap, cap), c])

    def own_mix(p, s):
        c = cols(out_parts, p)
        return spread(meta[s], pair(s, 0, cap, c).astype(bf16), y_in[s, own_slots, c])

    def gather(p, j):
        s = block_at(j)
        kind, c = out_parts[p][0], cols(out_parts, p)
        if kind == "A":
            arrived(x_in.at[s, :, c], px_r.at[p, s])
            y_out[s, own_slots, c] = (
                pair(s, group, cap, c) + x_in[s, pl.ds(cap, cap), c].astype(f32)
            ).astype(bf16)
            send(y_out.at[s, own_slots, c], y_in.at[s, own_slots, c],
                 py_s.at[p, s], py_r.at[p, s], y_peer)
            return
        arrived(y_in.at[s, :, c], py_r.at[p, s])
        if kind == "B":
            x_out[s, pl.ds(0, rows), c] = far_mix(p, s).astype(bf16)
            send(x_out.at[s, pl.ds(0, rows), c], x_in.at[s, pl.ds(0, rows), c],
                 px_s.at[p, s], px_r.at[p, s], x_peer)
        else:
            deliver(p, s, own_mix(p, s), far_mix(p, s))

    def comb(p, j):
        s = block_at(j)
        kind, c = out_parts[p][0], cols(out_parts, p)
        if kind == "A":
            arrived(y_in.at[s, own_slots, c], py_r.at[p, s])
            own = (pair(s, 0, cap, c) + x_in[s, own_slots, c].astype(f32)).astype(bf16)
            deliver(p, s, spread(meta[s], own, y_in[s, own_slots, c]))
        else:
            arrived(x_in.at[s, pl.ds(0, rows), c], px_r.at[p, s])
            deliver(p, s, own_mix(p, s) + x_in[s, pl.ds(0, rows), c].astype(f32))

    def chain(p, j):
        s = block_at(j)
        c, r = cols(out_parts, p), z_rows(p)

        @pl.when(joins(s))
        def _():
            arrived(mid_in.at[s, r, c], mi_r.at[p, s])
            z_out[s, r, c] = (z_out[s, r, c].astype(f32) + mid_in[s, r, c].astype(f32)).astype(bf16)

        z_send(p, s, joins(s))

    table = {
        "meta": greet, "relay": relay, "choose": choose, "forward": forward, "to_core": to_core,
        "up": up, "down": down, "core": core, "sum": gather, "comb": comb, "chain": chain,
    }

    for name, p, i in plan:
        table[name](p, i)

    def collect(p):
        kind, c = out_parts[p][0], cols(out_parts, p)
        for step in range(1, depth):
            q = ahead(step)

            @pl.when(jnp.logical_not(detour(q, z)))
            def _():
                arrived(z_in.at[q, z_rows(p), c], pz_r.at[p, q])
                acc[:, c] = acc[:, c] + z_in[q, pl.ds(0, rows), c].astype(f32)
                if kind == "C":
                    far_acc[:, c] = far_acc[:, c] + z_in[q, pl.ds(rows, rows), c].astype(f32)

    def leave(p):
        c = cols(out_parts, p)
        pltpu.make_async_copy(done.at[:, c], out.at[:, c], out_sem.at[p]).start()

    crossing = [p for p, (kind, _, _) in enumerate(out_parts) if kind == "C"]
    for p in crossing:
        c = cols(out_parts, p)
        collect(p)
        last_out[:, c] = far_acc[:, c].astype(bf16)
        send(last_out.at[:, c], last_in.at[:, c], last_s.at[p], last_r.at[p], x_peer)
    for p in range(len(out_parts)):
        if p not in crossing:
            c = cols(out_parts, p)
            collect(p)
            done[:, c] = acc[:, c].astype(bf16)
            leave(p)
    for p in crossing:
        c = cols(out_parts, p)
        arrived(last_in.at[:, c], last_r.at[p])
        done[:, c] = (acc[:, c] + last_in[:, c].astype(f32)).astype(bf16)
        leave(p)

    arrived(meta.at[0], fx_s.at[0])
    for p in crossing:
        arrived(last_out.at[:, cols(out_parts, p)], last_s.at[p])

    def settle(s, carry):
        passed(s, meta.at[s], m_s.at[0, s], m_s.at[1, s])
        passed(s, far_meta.at[s], fm_s.at[0, s], fm_s.at[1, s])
        for p, (kind, _, _) in enumerate(in_parts):
            c = cols(in_parts, p)
            passed(s, tok.at[s, :, c], zt_s.at[p, 0, s], zt_s.at[p, 1, s])
            if kind == "C":
                passed(s, far_tok.at[s, :, c], zf_s.at[p, 0, s], zf_s.at[p, 1, s])
            if kind != "A":
                @pl.when((s == z) | (kind == "B"))
                def _():
                    arrived(far_tok.at[s, :, c], raw_s.at[p, s])

                arrived(y_pick.at[s, :, c], yp_s.at[p, s])
            else:
                slab = x_buf.at[s, own_slots, c]
                for sem in (yp_s, xa_s, xb_s):
                    arrived(slab, sem.at[p, s])
            arrived(x_buf.at[s, mine, c], cc_s.at[p, s])
        for p, (kind, _, _) in enumerate(out_parts):
            c = cols(out_parts, p)
            arrived(c_in.at[s, :, c], pc_s.at[p, s])
            if kind == "A":
                arrived(x_out.at[s, :, c], px_s.at[p, s])
                arrived(y_out.at[s, own_slots, c], py_s.at[p, s])
            else:
                arrived(y_out.at[s, :, c], py_s.at[p, s])
                if kind == "B":
                    arrived(x_out.at[s, pl.ds(0, rows), c], px_s.at[p, s])

            @pl.when(s != z)
            def _():
                arrived(z_out.at[s, z_rows(p), c], pz_s.at[p, s])
        return carry

    lax.fori_loop(0, depth, settle, 0)
    for p in range(len(out_parts)):
        arrived(done.at[:, cols(out_parts, p)], out_sem.at[p])


IN_PARTS = (("A", 0), ("A", 1152), ("C", 2048))
OUT_PARTS = (("A", 0), ("A", 896), ("C", 1920), ("C", 2432))
PLAN = (
    ("meta", 0, 0), ("choose", 0, 0), ("choose", 1, 0), ("forward", 0, 0), ("choose", 2, 0),
    ("relay", 1, 1), ("forward", 1, 0), ("meta", 0, 1), ("choose", 1, 1), ("to_core", 0, 0),
    ("to_core", 2, 0), ("relay", 0, 1), ("choose", 0, 1), ("relay", 2, 1), ("choose", 2, 1),
    ("to_core", 1, 0), ("forward", 1, 1), ("up", 0, 0), ("relay", 1, 2), ("forward", 0, 1),
    ("meta", 0, 2), ("up", 1, 0), ("relay", 0, 2), ("choose", 0, 2), ("up", 2, 0),
    ("to_core", 1, 1), ("choose", 1, 2), ("down", 2, 0), ("down", 3, 0), ("to_core", 2, 1),
    ("meta", 0, 3), ("relay", 2, 2), ("choose", 2, 2), ("to_core", 0, 1), ("down", 0, 0),
    ("forward", 0, 2), ("relay", 1, 3), ("choose", 1, 3), ("down", 1, 0), ("up", 0, 1),
    ("forward", 1, 2), ("relay", 0, 3), ("choose", 0, 3), ("up", 1, 1), ("up", 2, 1),
    ("down", 3, 1), ("to_core", 2, 2), ("down", 0, 1), ("to_core", 0, 2), ("forward", 1, 3),
    ("relay", 2, 3), ("forward", 0, 3), ("to_core", 1, 2), ("choose", 2, 3), ("down", 2, 1),
    ("down", 1, 1), ("core", 0, 1), ("up", 0, 2), ("to_core", 1, 3), ("core", 2, 1),
    ("core", 1, 0), ("up", 1, 2), ("up", 2, 2), ("core", 3, 1), ("down", 2, 2), ("down", 0, 2),
    ("sum", 2, 1), ("core", 2, 2), ("to_core", 2, 3), ("core", 2, 0), ("sum", 0, 1),
    ("to_core", 0, 3), ("down", 1, 2), ("core", 0, 2), ("down", 3, 2), ("sum", 3, 1),
    ("up", 0, 3), ("sum", 2, 2), ("up", 1, 3), ("core", 1, 2), ("up", 2, 3), ("sum", 0, 2),
    ("comb", 0, 1), ("down", 1, 3), ("core", 3, 2), ("down", 3, 3), ("down", 2, 3),
    ("core", 1, 3), ("comb", 0, 2), ("core", 3, 3), ("chain", 2, 1), ("core", 2, 3),
    ("down", 0, 3), ("sum", 3, 2), ("core", 0, 3), ("sum", 1, 2), ("sum", 3, 3), ("core", 1, 1),
    ("core", 0, 0), ("chain", 0, 1), ("chain", 3, 2), ("sum", 1, 3), ("sum", 2, 3),
    ("chain", 3, 1), ("sum", 0, 3), ("chain", 0, 2), ("chain", 3, 3), ("sum", 1, 0),
    ("comb", 1, 3), ("core", 3, 0), ("comb", 0, 3), ("comb", 1, 2), ("chain", 1, 2),
    ("chain", 2, 3), ("sum", 1, 1), ("chain", 1, 3), ("chain", 2, 2), ("sum", 0, 0),
    ("sum", 3, 0), ("sum", 2, 0), ("chain", 0, 3), ("comb", 1, 0), ("comb", 1, 1),
    ("chain", 1, 1), ("comb", 0, 0),
)


def gathered_plan(tokens, expert_ids, gate_codes, w_gate, w_up, w_down, capacity, expert_count):
    rows, top = expert_ids.shape
    width = tokens.shape[1]
    w_gate, w_up = jnp.swapaxes(w_gate, 1, 2), jnp.swapaxes(w_up, 1, 2)
    part_width = w_gate.shape[1]
    depth = lax.axis_size("expert") // 2
    f32, bf16 = jnp.float32, jnp.bfloat16
    group = 2 * capacity
    vm, dma = pltpu.VMEM, pltpu.SemaphoreType.DMA

    def bounds(parts):
        lows = [low for _, low in parts]
        return [(kind, low, high) for (kind, low), high in zip(parts, lows[1:] + [width])]

    in_parts, out_parts = bounds(IN_PARTS), bounds(OUT_PARTS)
    ins, outs = len(in_parts), len(out_parts)
    two, one = dma((ins, 2, depth)), dma((ins, depth))
    block = vm((depth, group, width), bf16)
    pair = vm((depth, 2 * rows, width), bf16)
    return pl.pallas_call(
        functools.partial(fused, depth, expert_count, capacity, in_parts, out_parts, PLAN),
        out_shape=jax.ShapeDtypeStruct((rows, width), bf16),
        in_specs=[pl.BlockSpec(memory_space=pl.ANY)] * 6,
        out_specs=pl.BlockSpec(memory_space=pl.ANY),
        scratch_shapes=[
            vm((top, rows), jnp.int32),
            vm((top, rows), jnp.int32),
            vm((rows, width), bf16),
            vm((depth, rows, width), bf16),
            vm((depth, rows, width), bf16),
            vm((depth, 2 * expert_count, rows), f32),
            vm((depth, 2 * expert_count, rows), f32),
            block,
            vm((depth, 4 * group, width), bf16),
            vm(w_gate.shape[1:], bf16),
            vm(w_up.shape[1:], bf16),
            vm(w_down.shape[1:], bf16),
            vm((4 * group, part_width), bf16),
            vm((depth, 4 * group, width), bf16),
            vm((depth, 2 * group, width), bf16),
            block,
            block,
            block,
            block,
            pair,
            pair,
            pair,
            vm((rows, width), f32),
            vm((rows, width), f32),
            vm((rows, width), bf16),
            vm((rows, width), bf16),
            dma((6,)),
            dma((outs,)),
            dma((2, depth)),
            dma((depth,)),
            dma((2, depth)),
            dma((depth,)),
            dma((1,)),
            two,
            one,
            two,
        ]
        + [one] * 11
        + [dma((outs, depth))] * 9
        + [dma((outs,))] * 2,
        compiler_params=pltpu.CompilerParams(
            collective_id=0, has_side_effects=True, vmem_limit_bytes=63 << 20
        ),
    )(tokens, expert_ids.T, gate_codes.T, w_gate, w_up, w_down)


def slot_plan(tokens, expert_ids, gate_codes, w_gate, w_up, w_down):
    tok_rows, top_count = expert_ids.shape
    width = tokens.shape[1]
    expert_count = lax.axis_size("expert") * w_gate.shape[0]
    capacity = 3 * tok_rows * top_count // (2 * expert_count)
    slot_count = expert_count * capacity
    flat_ids = expert_ids.reshape(-1)
    onehot = (flat_ids[:, None] == jnp.arange(expert_count, dtype=jnp.int32)[None, :]).astype(
        jnp.int32
    )
    ranking = jnp.sum((jnp.cumsum(onehot, axis=0) - 1) * onehot, axis=1)
    target = flat_ids * capacity + ranking
    picker = (target[:, None] == jnp.arange(slot_count, dtype=jnp.int32)[None, :]).astype(
        jnp.bfloat16
    )
    selector = jnp.sum(picker.reshape(tok_rows, top_count, slot_count), axis=1)
    outgoing = jnp.einsum("ts,td->sd", selector, tokens, preferred_element_type=jnp.float32).astype(
        jnp.bfloat16
    )
    arrived = lax.all_to_all(outgoing, "expert", split_axis=0, concat_axis=0, tiled=True)
    gathered = lax.all_gather(arrived, "replica", axis=0, tiled=True)
    gate = jnp.dot(gathered, w_gate[0], preferred_element_type=jnp.float32)
    up = jnp.dot(gathered, w_up[0], preferred_element_type=jnp.float32)
    hidden = activate(gate, up).astype(jnp.bfloat16)
    summed = lax.psum_scatter(
        jnp.dot(hidden, w_down[0], preferred_element_type=jnp.float32).astype(jnp.bfloat16),
        "replica",
        scatter_dimension=0,
        tiled=True,
    )
    returned = lax.all_to_all(summed, "expert", split_axis=0, concat_axis=0, tiled=True)
    per_choice = jnp.dot(picker, returned, preferred_element_type=jnp.float32)
    gates = gate_codes.astype(jnp.float32) / 65536.0
    weighted = per_choice.reshape(tok_rows, top_count, width) * gates[:, :, None]
    return jnp.sum(weighted, axis=1).astype(jnp.bfloat16)


def on_device(tokens, expert_ids, gate_codes, w_gate, w_up, w_down):
    rows, top = expert_ids.shape
    expert_count = lax.axis_size("expert") * w_gate.shape[0]
    capacity = 3 * rows * top // (2 * expert_count)
    args = (tokens, expert_ids, gate_codes, w_gate, w_up, w_down)
    paired = w_gate.shape[0] == 1 and lax.axis_size("replica") == 2 * CORES
    if paired and 2 * capacity > rows:
        return gathered_plan(*args, capacity, expert_count)
    return slot_plan(*args)


def solution(mesh):
    return jax.shard_map(
        on_device,
        mesh=mesh,
        in_specs=(
            P(("expert", "replica"), None),
            P(("expert", "replica"), None),
            P(("expert", "replica"), None),
            P("expert", None, "replica"),
            P("expert", None, "replica"),
            P("expert", "replica", None),
        ),
        out_specs=P(("expert", "replica"), None),
        check_vma=False,
    )
```

```python
import functools

import jax
import jax.numpy as jnp
from jax import lax
from jax.experimental import pallas as pl
from jax.experimental.pallas import tpu as pltpu
from jax.sharding import PartitionSpec as P

MESH = pl.DeviceIdType.MESH
CORES = 2


def activate(gate, up):
    return gate * jax.nn.sigmoid(1.702 * gate) * (up + 1.0)


def spans(extent, step):
    return [(low, min(low + step, extent)) for low in range(0, extent, step)]


def fused(
    depth, experts, cap, in_parts, out_parts, plan,
    tokens, ids_in, codes_in, w_gate, w_up, w_down, out,
    ids, codes, done, tok, far_tok, meta, far_meta, y_pick, x_buf, wg, wu, wd, hid, part, c_in,
    x_out, x_in, y_out, y_in, z_out, z_in, mid_in, acc, far_acc, last_out, last_in,
    w_sem, out_sem, m_s, m_r, fm_s, fm_r, fx_s,
    zt_s, zt_r, zf_s, zf_r, raw_s, raw_r, yp_s, yp_r, xa_s, xa_r, xb_s, xb_r, cc_s, cc_r,
    pc_s, pc_r, px_s, px_r, py_s, py_r, pz_s, pz_r, mi_r, last_s, last_r,
):
    rows, width = tokens.shape
    f32, bf16 = jnp.float32, jnp.bfloat16
    expert, replica = lax.axis_index("expert"), lax.axis_index("replica")
    z, y = expert // 2, expert % 2
    other = z * 2 + (1 - y)
    y_peer = {"expert": other}
    x_peer = {"replica": (replica + CORES) % (2 * CORES)}
    c_peer = {"replica": replica // CORES * CORES + (1 - replica % CORES)}
    group = 2 * cap
    own_slots, mine = pl.ds(0, cap), pl.ds(0, 2 * group)

    def z_peer(level):
        return {"expert": level * 2 + y}

    def ahead(step):
        return (z + step) % depth

    def send(src, dst, ssem, rsem, peer):
        pltpu.make_async_remote_copy(
            src_ref=src, dst_ref=dst, send_sem=ssem, recv_sem=rsem,
            device_id=peer, device_id_type=MESH,
        ).start()

    def arrived(dst, sem):
        pltpu.make_async_copy(dst, dst, sem).wait()

    def block_at(i):
        pairs = jnp.minimum(z, depth - 1 - z)
        inward = jnp.where(2 * z < depth, 1, -1)
        beside = jnp.where(i % 2 == 1, z + inward * ((i + 1) // 2), z - inward * (i // 2))
        beyond = jnp.where(2 * z < depth, i, depth - 1 - i)
        return jnp.where(i <= 2 * pairs, beside, beyond)

    def cols(parts, p):
        _, low, high = parts[p]
        return pl.ds(low, high - low)

    barrier = pltpu.get_barrier_semaphore()
    for peer in (y_peer, x_peer, c_peer):
        pl.semaphore_signal(barrier, inc=1, device_id=peer, device_id_type=MESH)
    for inside, step in ((z < depth - 1, 1), (z > 0, depth - 1)):
        @pl.when(inside)
        def _():
            pl.semaphore_signal(
                barrier, inc=1, device_id=z_peer(ahead(step)), device_id_type=MESH
            )

    neighbours = 3 + jnp.where(z < depth - 1, 1, 0) + jnp.where(z > 0, 1, 0)
    own_load = pltpu.make_async_copy(tokens, tok.at[z], w_sem.at[3])
    id_load = pltpu.make_async_copy(ids_in, ids, w_sem.at[4])
    code_load = pltpu.make_async_copy(codes_in, codes, w_sem.at[5])
    for load in (own_load, id_load, code_load):
        load.start()
    loads = [
        pltpu.make_async_copy(src.at[0], dst, w_sem.at[i])
        for i, (src, dst) in enumerate(((w_gate, wg), (w_up, wu), (w_down, wd)))
    ]
    for load in loads:
        load.start()

    pl.semaphore_wait(barrier, neighbours)
    own_load.wait()

    def upward(s):
        return (s <= z) & (z < depth - 1)

    def downward(s):
        return (s >= z) & (z > 0)

    def pass_on(s, src, up_sem, down_sem, rsem):
        @pl.when(upward(s))
        def _():
            send(src, src, up_sem, rsem, z_peer(ahead(1)))

        @pl.when(downward(s))
        def _():
            send(src, src, down_sem, rsem, z_peer(ahead(depth - 1)))

    def passed(s, src, up_sem, down_sem):
        @pl.when(upward(s))
        def _():
            arrived(src, up_sem)

        @pl.when(downward(s))
        def _():
            arrived(src, down_sem)

    def pass_tok(p, s):
        pass_on(s, tok.at[s, :, cols(in_parts, p)], zt_s.at[p, 0, s], zt_s.at[p, 1, s], zt_r.at[p, s])

    def pass_far(p, s):
        pass_on(s, far_tok.at[s, :, cols(in_parts, p)], zf_s.at[p, 0, s], zf_s.at[p, 1, s], zf_r.at[p, s])

    def send_raw(p, s):
        c = cols(in_parts, p)
        send(tok.at[s, :, c], far_tok.at[s, :, c], raw_s.at[p, s], raw_r.at[p, s], x_peer)

    pass_tok(0, z)
    id_load.wait()
    code_load.wait()
    label = lax.broadcasted_iota(jnp.int32, (experts, rows), 0)
    named = jnp.zeros((experts, rows), f32)
    weight = jnp.zeros((experts, rows), f32)
    for k in range(ids.shape[0]):
        same = label == ids[k : k + 1, :]
        named = named + jnp.where(same, 1.0, 0.0)
        weight = weight + jnp.where(same, codes[k : k + 1, :].astype(f32) / 65536.0, 0.0)
    upto = lax.broadcasted_iota(jnp.int32, (rows, rows), 0) <= lax.broadcasted_iota(
        jnp.int32, (rows, rows), 1
    )
    counts = jnp.dot(
        named.astype(bf16), jnp.where(upto, 1.0, 0.0).astype(bf16), preferred_element_type=f32
    )
    meta[z, pl.ds(0, experts), :] = jnp.where(named > 0, counts - 1.0, -1.0)
    meta[z, pl.ds(experts, experts), :] = weight
    send(meta.at[z], far_meta.at[z], fx_s.at[0], fm_r.at[z], x_peer)
    pass_on(z, meta.at[z], m_s.at[0, z], m_s.at[1, z], m_r.at[z])
    for p in range(1, len(in_parts)):
        pass_tok(p, z)
    for p, (kind, _, _) in enumerate(in_parts):
        if kind != "A":
            send_raw(p, z)

    def row_of(table, which):
        sub = lax.broadcasted_iota(jnp.int32, table.shape, 0)
        return jnp.sum(jnp.where(sub == which, table, 0.0), axis=0, keepdims=True)

    def slots(table, which):
        slot = lax.broadcasted_iota(jnp.int32, (cap, rows), 0).astype(f32)
        return slot == row_of(table, which)

    def picker(table):
        return jnp.concatenate(
            [jnp.where(slots(table, e), 1.0, 0.0) for e in (expert, other)], axis=0
        ).astype(bf16)

    def spreader(table):
        high, low = [], []
        for e in (expert, other):
            share = row_of(table, e + experts)
            coarse = share.astype(bf16).astype(f32)
            here = slots(table, e)
            high.append(jnp.where(here, coarse, 0.0))
            low.append(jnp.where(here, share - coarse, 0.0))
        return jnp.concatenate(high + low, axis=0).astype(bf16)

    def spread(table, own, far):
        stacked = jnp.concatenate([own, far, own, far], axis=0)
        return lax.dot_general(
            spreader(table), stacked, (((0,), (0,)), ((), ())), preferred_element_type=f32
        )

    def greet(p, i):
        s = block_at(i)

        @pl.when(i > 0)
        def _():
            arrived(meta.at[s], m_r.at[s])
            pass_on(s, meta.at[s], m_s.at[0, s], m_s.at[1, s], m_r.at[s])

        arrived(far_meta.at[s], fm_r.at[s])
        pass_on(s, far_meta.at[s], fm_s.at[0, s], fm_s.at[1, s], fm_r.at[s])

    def relay(p, i):
        s = block_at(i)
        kind, c = in_parts[p][0], cols(in_parts, p)
        arrived(tok.at[s, :, c], zt_r.at[p, s])
        pass_tok(p, s)
        if kind == "C":
            arrived(far_tok.at[s, :, c], zf_r.at[p, s])
            pass_far(p, s)
        if kind == "B":
            send_raw(p, s)

    def choose(p, i):
        s = block_at(i)
        kind, c = in_parts[p][0], cols(in_parts, p)

        def pick(table, block, low):
            chosen = jnp.dot(picker(table[s]), block[s, :, c], preferred_element_type=f32).astype(bf16)
            x_buf[s, pl.ds(low, cap), c] = chosen[:cap]
            y_pick[s, pl.ds(low, cap), c] = chosen[cap:]

        if kind == "A":
            pick(meta, tok, 0)
            send(y_pick.at[s, own_slots, c], x_buf.at[s, pl.ds(group, cap), c],
                 yp_s.at[p, s], yp_r.at[p, s], y_peer)
            send(x_buf.at[s, own_slots, c], x_buf.at[s, pl.ds(cap, cap), c],
                 xa_s.at[p, s], xa_r.at[p, s], x_peer)
            return

        @pl.when((i == 0) | (kind == "B"))
        def _():
            arrived(far_tok.at[s, :, c], raw_r.at[p, s])
            if kind == "C":
                pass_far(p, s)

        pick(meta, tok, 0)
        pick(far_meta, far_tok, cap)
        send(y_pick.at[s, :, c], x_buf.at[s, pl.ds(group, group), c],
             yp_s.at[p, s], yp_r.at[p, s], y_peer)

    def forward(p, i):
        s = block_at(i)
        c = cols(in_parts, p)
        here = x_buf.at[s, pl.ds(group, cap), c]
        arrived(here, yp_r.at[p, s])
        send(here, x_buf.at[s, pl.ds(group + cap, cap), c], xb_s.at[p, s], xb_r.at[p, s], x_peer)

    def to_core(p, i):
        s = block_at(i)
        kind, c = in_parts[p][0], cols(in_parts, p)
        if kind == "A":
            arrived(x_buf.at[s, pl.ds(cap, cap), c], xa_r.at[p, s])
            arrived(x_buf.at[s, pl.ds(group + cap, cap), c], xb_r.at[p, s])
        else:
            arrived(x_buf.at[s, pl.ds(group, group), c], yp_r.at[p, s])
        send(x_buf.at[s, mine, c], x_buf.at[s, pl.ds(2 * group, 2 * group), c],
             cc_s.at[p, s], cc_r.at[p, s], c_peer)

    first_up = next(i for name, _, i in plan if name == "up")
    ups = sum(1 for name, _, i in plan if name == "up" and i == first_up)
    pieces = spans(wg.shape[0], 256)

    def up(p, i):
        s = block_at(i)
        if p == 0:
            for q in range(len(in_parts)):
                arrived(x_buf.at[s, mine, cols(in_parts, q)], cc_r.at[q, s])

            @pl.when(i == first_up)
            def _():
                for load in loads:
                    load.wait()

        across = (((1,), (1,)), ((), ()))
        for low, high in pieces if ups == 1 else pieces[p::ups]:
            block = x_buf[s]
            gate = lax.dot_general(block, wg[low:high, :], across, preferred_element_type=f32)
            more = lax.dot_general(block, wu[low:high, :], across, preferred_element_type=f32)
            hid[:, low:high] = activate(gate, more).astype(bf16)

    def down(p, i):
        s = block_at(i)
        _, start, stop = out_parts[p]
        for low, high in spans(stop - start, 512):
            here = slice(start + low, start + high)
            part[s, :, here] = jnp.dot(
                hid[...], wd[:, here], preferred_element_type=f32
            ).astype(bf16)
        c = cols(out_parts, p)
        send(part.at[s, pl.ds(2 * group, 2 * group), c], c_in.at[s, :, c],
             pc_s.at[p, s], pc_r.at[p, s], c_peer)

    def pair(s, low, count, c):
        return part[s, pl.ds(low, count), c].astype(f32) + c_in[s, pl.ds(low, count), c].astype(f32)

    def core(p, j):
        s = block_at(j)
        kind, c = out_parts[p][0], cols(out_parts, p)
        arrived(c_in.at[s, :, c], pc_r.at[p, s])
        if kind == "A":
            for n in range(2):
                x_out[s, pl.ds(n * cap, cap), c] = pair(s, cap + n * group, cap, c).astype(bf16)
            send(x_out.at[s, :, c], x_in.at[s, :, c], px_s.at[p, s], px_r.at[p, s], x_peer)
        else:
            y_out[s, :, c] = pair(s, group, group, c).astype(bf16)
            send(y_out.at[s, :, c], y_in.at[s, :, c], py_s.at[p, s], py_r.at[p, s], y_peer)

    def detour(source, owner):
        return ((source == 0) & (owner > 1)) | ((source == depth - 1) & (owner < depth - 2))

    def joins(s):
        return ((z == 1) & (s > 1)) | ((z == depth - 2) & (s < depth - 2))

    def z_rows(p):
        return pl.ds(0, 2 * rows if out_parts[p][0] == "C" else rows)

    def z_send(p, s, ready):
        c, r = cols(out_parts, p), z_rows(p)

        @pl.when(ready & detour(z, s))
        def _():
            send(z_out.at[s, r, c], mid_in.at[s, r, c], pz_s.at[p, s], mi_r.at[p, s],
                 z_peer(jnp.where(z == 0, 1, depth - 2)))

        @pl.when(ready & jnp.logical_not(detour(z, s)))
        def _():
            send(z_out.at[s, r, c], z_in.at[z, r, c], pz_s.at[p, s], pz_r.at[p, z], z_peer(s))

    def deliver(p, s, total, far=None):
        c = cols(out_parts, p)

        @pl.when(s == z)
        def _():
            acc[:, c] = total
            if far is not None:
                far_acc[:, c] = far

        @pl.when(s != z)
        def _():
            z_out[s, pl.ds(0, rows), c] = total.astype(bf16)
            if far is not None:
                z_out[s, pl.ds(rows, rows), c] = far.astype(bf16)

        z_send(p, s, (s != z) & jnp.logical_not(joins(s)))

    def far_mix(p, s):
        c = cols(out_parts, p)
        return spread(far_meta[s], pair(s, cap, cap, c).astype(bf16), y_in[s, pl.ds(cap, cap), c])

    def own_mix(p, s):
        c = cols(out_parts, p)
        return spread(meta[s], pair(s, 0, cap, c).astype(bf16), y_in[s, own_slots, c])

    def gather(p, j):
        s = block_at(j)
        kind, c = out_parts[p][0], cols(out_parts, p)
        if kind == "A":
            arrived(x_in.at[s, :, c], px_r.at[p, s])
            y_out[s, own_slots, c] = (
                pair(s, group, cap, c) + x_in[s, pl.ds(cap, cap), c].astype(f32)
            ).astype(bf16)
            send(y_out.at[s, own_slots, c], y_in.at[s, own_slots, c],
                 py_s.at[p, s], py_r.at[p, s], y_peer)
            return
        arrived(y_in.at[s, :, c], py_r.at[p, s])
        if kind == "B":
            x_out[s, pl.ds(0, rows), c] = far_mix(p, s).astype(bf16)
            send(x_out.at[s, pl.ds(0, rows), c], x_in.at[s, pl.ds(0, rows), c],
                 px_s.at[p, s], px_r.at[p, s], x_peer)
        else:
            deliver(p, s, own_mix(p, s), far_mix(p, s))

    def comb(p, j):
        s = block_at(j)
        kind, c = out_parts[p][0], cols(out_parts, p)
        if kind == "A":
            arrived(y_in.at[s, own_slots, c], py_r.at[p, s])
            own = (pair(s, 0, cap, c) + x_in[s, own_slots, c].astype(f32)).astype(bf16)
            deliver(p, s, spread(meta[s], own, y_in[s, own_slots, c]))
        else:
            arrived(x_in.at[s, pl.ds(0, rows), c], px_r.at[p, s])
            deliver(p, s, own_mix(p, s) + x_in[s, pl.ds(0, rows), c].astype(f32))

    def chain(p, j):
        s = block_at(j)
        c, r = cols(out_parts, p), z_rows(p)

        @pl.when(joins(s))
        def _():
            arrived(mid_in.at[s, r, c], mi_r.at[p, s])
            z_out[s, r, c] = (z_out[s, r, c].astype(f32) + mid_in[s, r, c].astype(f32)).astype(bf16)

        z_send(p, s, joins(s))

    table = {
        "meta": greet, "relay": relay, "choose": choose, "forward": forward, "to_core": to_core,
        "up": up, "down": down, "core": core, "sum": gather, "comb": comb, "chain": chain,
    }

    for name, p, i in plan:
        table[name](p, i)

    def collect(p):
        kind, c = out_parts[p][0], cols(out_parts, p)
        for step in range(1, depth):
            q = ahead(step)

            @pl.when(jnp.logical_not(detour(q, z)))
            def _():
                arrived(z_in.at[q, z_rows(p), c], pz_r.at[p, q])
                acc[:, c] = acc[:, c] + z_in[q, pl.ds(0, rows), c].astype(f32)
                if kind == "C":
                    far_acc[:, c] = far_acc[:, c] + z_in[q, pl.ds(rows, rows), c].astype(f32)

    def leave(p):
        c = cols(out_parts, p)
        pltpu.make_async_copy(done.at[:, c], out.at[:, c], out_sem.at[p]).start()

    crossing = [p for p, (kind, _, _) in enumerate(out_parts) if kind == "C"]
    for p in crossing:
        c = cols(out_parts, p)
        collect(p)
        last_out[:, c] = far_acc[:, c].astype(bf16)
        send(last_out.at[:, c], last_in.at[:, c], last_s.at[p], last_r.at[p], x_peer)
    for p in range(len(out_parts)):
        if p not in crossing:
            c = cols(out_parts, p)
            collect(p)
            done[:, c] = acc[:, c].astype(bf16)
            leave(p)
    for p in crossing:
        c = cols(out_parts, p)
        arrived(last_in.at[:, c], last_r.at[p])
        done[:, c] = (acc[:, c] + last_in[:, c].astype(f32)).astype(bf16)
        leave(p)

    arrived(meta.at[0], fx_s.at[0])
    for p in crossing:
        arrived(last_out.at[:, cols(out_parts, p)], last_s.at[p])

    def settle(s, carry):
        passed(s, meta.at[s], m_s.at[0, s], m_s.at[1, s])
        passed(s, far_meta.at[s], fm_s.at[0, s], fm_s.at[1, s])
        for p, (kind, _, _) in enumerate(in_parts):
            c = cols(in_parts, p)
            passed(s, tok.at[s, :, c], zt_s.at[p, 0, s], zt_s.at[p, 1, s])
            if kind == "C":
                passed(s, far_tok.at[s, :, c], zf_s.at[p, 0, s], zf_s.at[p, 1, s])
            if kind != "A":
                @pl.when((s == z) | (kind == "B"))
                def _():
                    arrived(far_tok.at[s, :, c], raw_s.at[p, s])

                arrived(y_pick.at[s, :, c], yp_s.at[p, s])
            else:
                slab = x_buf.at[s, own_slots, c]
                for sem in (yp_s, xa_s, xb_s):
                    arrived(slab, sem.at[p, s])
            arrived(x_buf.at[s, mine, c], cc_s.at[p, s])
        for p, (kind, _, _) in enumerate(out_parts):
            c = cols(out_parts, p)
            arrived(c_in.at[s, :, c], pc_s.at[p, s])
            if kind == "A":
                arrived(x_out.at[s, :, c], px_s.at[p, s])
                arrived(y_out.at[s, own_slots, c], py_s.at[p, s])
            else:
                arrived(y_out.at[s, :, c], py_s.at[p, s])
                if kind == "B":
                    arrived(x_out.at[s, pl.ds(0, rows), c], px_s.at[p, s])

            @pl.when(s != z)
            def _():
                arrived(z_out.at[s, z_rows(p), c], pz_s.at[p, s])
        return carry

    lax.fori_loop(0, depth, settle, 0)
    for p in range(len(out_parts)):
        arrived(done.at[:, cols(out_parts, p)], out_sem.at[p])


IN_PARTS = (("A", 0), ("A", 1024), ("C", 2176))
OUT_PARTS = (("A", 0), ("A", 896), ("C", 1920), ("C", 2432))
PLAN = (
    ("meta", 0, 0), ("choose", 0, 0), ("choose", 1, 0), ("choose", 2, 0), ("forward", 0, 0),
    ("relay", 0, 1), ("forward", 1, 0), ("meta", 0, 1), ("choose", 0, 1), ("relay", 1, 1),
    ("to_core", 0, 0), ("to_core", 2, 0), ("relay", 2, 1), ("choose", 1, 1), ("to_core", 1, 0),
    ("meta", 0, 2), ("choose", 2, 1), ("forward", 0, 1), ("relay", 0, 2), ("up", 0, 0),
    ("forward", 1, 1), ("choose", 0, 2), ("up", 1, 0), ("up", 2, 0), ("to_core", 2, 1),
    ("relay", 1, 2), ("choose", 1, 2), ("down", 2, 0), ("to_core", 0, 1), ("meta", 0, 3),
    ("relay", 2, 2), ("choose", 2, 2), ("forward", 0, 2), ("relay", 0, 3), ("choose", 0, 3),
    ("core", 2, 0), ("to_core", 1, 1), ("down", 0, 0), ("down", 1, 0), ("down", 3, 0),
    ("forward", 1, 2), ("relay", 1, 3), ("choose", 1, 3), ("up", 0, 1), ("up", 1, 1),
    ("to_core", 2, 2), ("up", 2, 1), ("to_core", 0, 2), ("down", 3, 1), ("forward", 0, 3),
    ("relay", 2, 3), ("choose", 2, 3), ("to_core", 1, 2), ("down", 0, 1), ("forward", 1, 3),
    ("down", 2, 1), ("core", 3, 1), ("core", 1, 0), ("down", 1, 1), ("up", 0, 2),
    ("to_core", 0, 3), ("up", 1, 2), ("core", 2, 1), ("to_core", 1, 3), ("up", 2, 2),
    ("to_core", 2, 3), ("core", 0, 1), ("down", 2, 2), ("down", 0, 2), ("sum", 3, 1),
    ("down", 3, 2), ("sum", 2, 1), ("core", 2, 2), ("down", 1, 2), ("core", 0, 2), ("up", 0, 3),
    ("up", 1, 3), ("core", 3, 2), ("sum", 0, 1), ("sum", 2, 2), ("core", 1, 2), ("up", 2, 3),
    ("down", 3, 3), ("down", 1, 3), ("sum", 3, 2), ("core", 3, 3), ("down", 2, 3), ("core", 1, 3),
    ("comb", 0, 1), ("chain", 2, 2), ("core", 2, 3), ("down", 0, 3), ("sum", 0, 2), ("sum", 3, 3),
    ("chain", 3, 1), ("sum", 1, 2), ("core", 0, 3), ("core", 0, 0), ("chain", 2, 1),
    ("sum", 2, 0), ("core", 1, 1), ("sum", 2, 3), ("sum", 1, 3), ("comb", 0, 2), ("chain", 3, 3),
    ("sum", 0, 3), ("comb", 1, 3), ("core", 3, 0), ("chain", 3, 2), ("sum", 1, 0),
    ("chain", 2, 3), ("comb", 0, 3), ("chain", 0, 2), ("chain", 0, 1), ("comb", 1, 2),
    ("sum", 0, 0), ("sum", 3, 0), ("chain", 1, 3), ("sum", 1, 1), ("comb", 1, 0), ("chain", 0, 3),
    ("comb", 0, 0), ("comb", 1, 1), ("chain", 1, 1), ("chain", 1, 2),
)


def gathered_plan(tokens, expert_ids, gate_codes, w_gate, w_up, w_down, capacity, expert_count):
    rows, top = expert_ids.shape
    width = tokens.shape[1]
    w_gate, w_up = jnp.swapaxes(w_gate, 1, 2), jnp.swapaxes(w_up, 1, 2)
    part_width = w_gate.shape[1]
    depth = lax.axis_size("expert") // 2
    f32, bf16 = jnp.float32, jnp.bfloat16
    group = 2 * capacity
    vm, dma = pltpu.VMEM, pltpu.SemaphoreType.DMA

    def bounds(parts):
        lows = [low for _, low in parts]
        return [(kind, low, high) for (kind, low), high in zip(parts, lows[1:] + [width])]

    in_parts, out_parts = bounds(IN_PARTS), bounds(OUT_PARTS)
    ins, outs = len(in_parts), len(out_parts)
    two, one = dma((ins, 2, depth)), dma((ins, depth))
    block = vm((depth, group, width), bf16)
    pair = vm((depth, 2 * rows, width), bf16)
    return pl.pallas_call(
        functools.partial(fused, depth, expert_count, capacity, in_parts, out_parts, PLAN),
        out_shape=jax.ShapeDtypeStruct((rows, width), bf16),
        in_specs=[pl.BlockSpec(memory_space=pl.ANY)] * 6,
        out_specs=pl.BlockSpec(memory_space=pl.ANY),
        scratch_shapes=[
            vm((top, rows), jnp.int32),
            vm((top, rows), jnp.int32),
            vm((rows, width), bf16),
            vm((depth, rows, width), bf16),
            vm((depth, rows, width), bf16),
            vm((depth, 2 * expert_count, rows), f32),
            vm((depth, 2 * expert_count, rows), f32),
            block,
            vm((depth, 4 * group, width), bf16),
            vm(w_gate.shape[1:], bf16),
            vm(w_up.shape[1:], bf16),
            vm(w_down.shape[1:], bf16),
            vm((4 * group, part_width), bf16),
            vm((depth, 4 * group, width), bf16),
            vm((depth, 2 * group, width), bf16),
            block,
            block,
            block,
            block,
            pair,
            pair,
            pair,
            vm((rows, width), f32),
            vm((rows, width), f32),
            vm((rows, width), bf16),
            vm((rows, width), bf16),
            dma((6,)),
            dma((outs,)),
            dma((2, depth)),
            dma((depth,)),
            dma((2, depth)),
            dma((depth,)),
            dma((1,)),
            two,
            one,
            two,
        ]
        + [one] * 11
        + [dma((outs, depth))] * 9
        + [dma((outs,))] * 2,
        compiler_params=pltpu.CompilerParams(
            collective_id=0, has_side_effects=True, vmem_limit_bytes=63 << 20
        ),
    )(tokens, expert_ids.T, gate_codes.T, w_gate, w_up, w_down)


def slot_plan(tokens, expert_ids, gate_codes, w_gate, w_up, w_down):
    tok_rows, top_count = expert_ids.shape
    width = tokens.shape[1]
    expert_count = lax.axis_size("expert") * w_gate.shape[0]
    capacity = 3 * tok_rows * top_count // (2 * expert_count)
    slot_count = expert_count * capacity
    flat_ids = expert_ids.reshape(-1)
    onehot = (flat_ids[:, None] == jnp.arange(expert_count, dtype=jnp.int32)[None, :]).astype(
        jnp.int32
    )
    ranking = jnp.sum((jnp.cumsum(onehot, axis=0) - 1) * onehot, axis=1)
    target = flat_ids * capacity + ranking
    picker = (target[:, None] == jnp.arange(slot_count, dtype=jnp.int32)[None, :]).astype(
        jnp.bfloat16
    )
    selector = jnp.sum(picker.reshape(tok_rows, top_count, slot_count), axis=1)
    outgoing = jnp.einsum("ts,td->sd", selector, tokens, preferred_element_type=jnp.float32).astype(
        jnp.bfloat16
    )
    arrived = lax.all_to_all(outgoing, "expert", split_axis=0, concat_axis=0, tiled=True)
    gathered = lax.all_gather(arrived, "replica", axis=0, tiled=True)
    gate = jnp.dot(gathered, w_gate[0], preferred_element_type=jnp.float32)
    up = jnp.dot(gathered, w_up[0], preferred_element_type=jnp.float32)
    hidden = activate(gate, up).astype(jnp.bfloat16)
    summed = lax.psum_scatter(
        jnp.dot(hidden, w_down[0], preferred_element_type=jnp.float32).astype(jnp.bfloat16),
        "replica",
        scatter_dimension=0,
        tiled=True,
    )
    returned = lax.all_to_all(summed, "expert", split_axis=0, concat_axis=0, tiled=True)
    per_choice = jnp.dot(picker, returned, preferred_element_type=jnp.float32)
    gates = gate_codes.astype(jnp.float32) / 65536.0
    weighted = per_choice.reshape(tok_rows, top_count, width) * gates[:, :, None]
    return jnp.sum(weighted, axis=1).astype(jnp.bfloat16)


def on_device(tokens, expert_ids, gate_codes, w_gate, w_up, w_down):
    rows, top = expert_ids.shape
    expert_count = lax.axis_size("expert") * w_gate.shape[0]
    capacity = 3 * rows * top // (2 * expert_count)
    args = (tokens, expert_ids, gate_codes, w_gate, w_up, w_down)
    paired = w_gate.shape[0] == 1 and lax.axis_size("replica") == 2 * CORES
    if paired and 2 * capacity > rows:
        return gathered_plan(*args, capacity, expert_count)
    return slot_plan(*args)


def solution(mesh):
    return jax.shard_map(
        on_device,
        mesh=mesh,
        in_specs=(
            P(("expert", "replica"), None),
            P(("expert", "replica"), None),
            P(("expert", "replica"), None),
            P("expert", None, "replica"),
            P("expert", None, "replica"),
            P("expert", "replica", None),
        ),
        out_specs=P(("expert", "replica"), None),
        check_vma=False,
    )
```

```python
import functools

import jax
import jax.numpy as jnp
from jax import lax
from jax.experimental import pallas as pl
from jax.experimental.pallas import tpu as pltpu
from jax.sharding import PartitionSpec as P

MESH = pl.DeviceIdType.MESH
CORES = 2


def activate(gate, up):
    return gate * jax.nn.sigmoid(1.702 * gate) * (up + 1.0)


def spans(extent, step):
    return [(low, min(low + step, extent)) for low in range(0, extent, step)]


def fused(
    depth, experts, cap, in_parts, out_parts, plan,
    tokens, ids_in, codes_in, w_gate, w_up, w_down, out,
    ids, codes, done, tok, far_tok, meta, far_meta, y_pick, x_buf, wg, wu, wd, hid, part, c_in,
    x_out, x_in, y_out, y_in, z_out, z_in, mid_in, acc, far_acc, last_out, last_in,
    w_sem, out_sem, m_s, m_r, fm_s, fm_r, fx_s,
    zt_s, zt_r, zf_s, zf_r, raw_s, raw_r, yp_s, yp_r, xa_s, xa_r, xb_s, xb_r, cc_s, cc_r,
    pc_s, pc_r, px_s, px_r, py_s, py_r, pz_s, pz_r, mi_r, last_s, last_r,
):
    rows, width = tokens.shape
    f32, bf16 = jnp.float32, jnp.bfloat16
    expert, replica = lax.axis_index("expert"), lax.axis_index("replica")
    z, y = expert // 2, expert % 2
    other = z * 2 + (1 - y)
    y_peer = {"expert": other}
    x_peer = {"replica": (replica + CORES) % (2 * CORES)}
    c_peer = {"replica": replica // CORES * CORES + (1 - replica % CORES)}
    group = 2 * cap
    own_slots, mine = pl.ds(0, cap), pl.ds(0, 2 * group)

    def z_peer(level):
        return {"expert": level * 2 + y}

    def ahead(step):
        return (z + step) % depth

    def send(src, dst, ssem, rsem, peer):
        pltpu.make_async_remote_copy(
            src_ref=src, dst_ref=dst, send_sem=ssem, recv_sem=rsem,
            device_id=peer, device_id_type=MESH,
        ).start()

    def arrived(dst, sem):
        pltpu.make_async_copy(dst, dst, sem).wait()

    def block_at(i):
        pairs = jnp.minimum(z, depth - 1 - z)
        inward = jnp.where(2 * z < depth, 1, -1)
        beside = jnp.where(i % 2 == 1, z + inward * ((i + 1) // 2), z - inward * (i // 2))
        beyond = jnp.where(2 * z < depth, i, depth - 1 - i)
        return jnp.where(i <= 2 * pairs, beside, beyond)

    def cols(parts, p):
        _, low, high = parts[p]
        return pl.ds(low, high - low)

    barrier = pltpu.get_barrier_semaphore()
    for peer in (y_peer, x_peer, c_peer):
        pl.semaphore_signal(barrier, inc=1, device_id=peer, device_id_type=MESH)
    for inside, step in ((z < depth - 1, 1), (z > 0, depth - 1)):
        @pl.when(inside)
        def _():
            pl.semaphore_signal(
                barrier, inc=1, device_id=z_peer(ahead(step)), device_id_type=MESH
            )

    neighbours = 3 + jnp.where(z < depth - 1, 1, 0) + jnp.where(z > 0, 1, 0)
    own_load = pltpu.make_async_copy(tokens, tok.at[z], w_sem.at[3])
    id_load = pltpu.make_async_copy(ids_in, ids, w_sem.at[4])
    code_load = pltpu.make_async_copy(codes_in, codes, w_sem.at[5])
    for load in (own_load, id_load, code_load):
        load.start()
    loads = [
        pltpu.make_async_copy(src.at[0], dst, w_sem.at[i])
        for i, (src, dst) in enumerate(((w_gate, wg), (w_up, wu), (w_down, wd)))
    ]
    for load in loads:
        load.start()

    pl.semaphore_wait(barrier, neighbours)
    own_load.wait()

    def upward(s):
        return (s <= z) & (z < depth - 1)

    def downward(s):
        return (s >= z) & (z > 0)

    def pass_on(s, src, up_sem, down_sem, rsem):
        @pl.when(upward(s))
        def _():
            send(src, src, up_sem, rsem, z_peer(ahead(1)))

        @pl.when(downward(s))
        def _():
            send(src, src, down_sem, rsem, z_peer(ahead(depth - 1)))

    def passed(s, src, up_sem, down_sem):
        @pl.when(upward(s))
        def _():
            arrived(src, up_sem)

        @pl.when(downward(s))
        def _():
            arrived(src, down_sem)

    def pass_tok(p, s):
        pass_on(s, tok.at[s, :, cols(in_parts, p)], zt_s.at[p, 0, s], zt_s.at[p, 1, s], zt_r.at[p, s])

    def pass_far(p, s):
        pass_on(s, far_tok.at[s, :, cols(in_parts, p)], zf_s.at[p, 0, s], zf_s.at[p, 1, s], zf_r.at[p, s])

    def send_raw(p, s):
        c = cols(in_parts, p)
        send(tok.at[s, :, c], far_tok.at[s, :, c], raw_s.at[p, s], raw_r.at[p, s], x_peer)

    pass_tok(0, z)
    id_load.wait()
    code_load.wait()
    label = lax.broadcasted_iota(jnp.int32, (experts, rows), 0)
    named = jnp.zeros((experts, rows), f32)
    weight = jnp.zeros((experts, rows), f32)
    for k in range(ids.shape[0]):
        same = label == ids[k : k + 1, :]
        named = named + jnp.where(same, 1.0, 0.0)
        weight = weight + jnp.where(same, codes[k : k + 1, :].astype(f32) / 65536.0, 0.0)
    upto = lax.broadcasted_iota(jnp.int32, (rows, rows), 0) <= lax.broadcasted_iota(
        jnp.int32, (rows, rows), 1
    )
    counts = jnp.dot(
        named.astype(bf16), jnp.where(upto, 1.0, 0.0).astype(bf16), preferred_element_type=f32
    )
    meta[z, pl.ds(0, experts), :] = jnp.where(named > 0, counts - 1.0, -1.0)
    meta[z, pl.ds(experts, experts), :] = weight
    send(meta.at[z], far_meta.at[z], fx_s.at[0], fm_r.at[z], x_peer)
    pass_on(z, meta.at[z], m_s.at[0, z], m_s.at[1, z], m_r.at[z])
    for p in range(1, len(in_parts)):
        pass_tok(p, z)
    for p, (kind, _, _) in enumerate(in_parts):
        if kind != "A":
            send_raw(p, z)

    def row_of(table, which):
        sub = lax.broadcasted_iota(jnp.int32, table.shape, 0)
        return jnp.sum(jnp.where(sub == which, table, 0.0), axis=0, keepdims=True)

    def slots(table, which):
        slot = lax.broadcasted_iota(jnp.int32, (cap, rows), 0).astype(f32)
        return slot == row_of(table, which)

    def picker(table):
        return jnp.concatenate(
            [jnp.where(slots(table, e), 1.0, 0.0) for e in (expert, other)], axis=0
        ).astype(bf16)

    def spreader(table):
        high, low = [], []
        for e in (expert, other):
            share = row_of(table, e + experts)
            coarse = share.astype(bf16).astype(f32)
            here = slots(table, e)
            high.append(jnp.where(here, coarse, 0.0))
            low.append(jnp.where(here, share - coarse, 0.0))
        return jnp.concatenate(high + low, axis=0).astype(bf16)

    def spread(table, own, far):
        stacked = jnp.concatenate([own, far, own, far], axis=0)
        return lax.dot_general(
            spreader(table), stacked, (((0,), (0,)), ((), ())), preferred_element_type=f32
        )

    def greet(p, i):
        s = block_at(i)

        @pl.when(i > 0)
        def _():
            arrived(meta.at[s], m_r.at[s])
            pass_on(s, meta.at[s], m_s.at[0, s], m_s.at[1, s], m_r.at[s])

        arrived(far_meta.at[s], fm_r.at[s])
        pass_on(s, far_meta.at[s], fm_s.at[0, s], fm_s.at[1, s], fm_r.at[s])

    def relay(p, i):
        s = block_at(i)
        kind, c = in_parts[p][0], cols(in_parts, p)
        arrived(tok.at[s, :, c], zt_r.at[p, s])
        pass_tok(p, s)
        if kind == "C":
            arrived(far_tok.at[s, :, c], zf_r.at[p, s])
            pass_far(p, s)
        if kind == "B":
            send_raw(p, s)

    def choose(p, i):
        s = block_at(i)
        kind, c = in_parts[p][0], cols(in_parts, p)

        def pick(table, block, low):
            chosen = jnp.dot(picker(table[s]), block[s, :, c], preferred_element_type=f32).astype(bf16)
            x_buf[s, pl.ds(low, cap), c] = chosen[:cap]
            y_pick[s, pl.ds(low, cap), c] = chosen[cap:]

        if kind == "A":
            pick(meta, tok, 0)
            send(y_pick.at[s, own_slots, c], x_buf.at[s, pl.ds(group, cap), c],
                 yp_s.at[p, s], yp_r.at[p, s], y_peer)
            send(x_buf.at[s, own_slots, c], x_buf.at[s, pl.ds(cap, cap), c],
                 xa_s.at[p, s], xa_r.at[p, s], x_peer)
            return

        @pl.when((i == 0) | (kind == "B"))
        def _():
            arrived(far_tok.at[s, :, c], raw_r.at[p, s])
            if kind == "C":
                pass_far(p, s)

        pick(meta, tok, 0)
        pick(far_meta, far_tok, cap)
        send(y_pick.at[s, :, c], x_buf.at[s, pl.ds(group, group), c],
             yp_s.at[p, s], yp_r.at[p, s], y_peer)

    def forward(p, i):
        s = block_at(i)
        c = cols(in_parts, p)
        here = x_buf.at[s, pl.ds(group, cap), c]
        arrived(here, yp_r.at[p, s])
        send(here, x_buf.at[s, pl.ds(group + cap, cap), c], xb_s.at[p, s], xb_r.at[p, s], x_peer)

    def to_core(p, i):
        s = block_at(i)
        kind, c = in_parts[p][0], cols(in_parts, p)
        if kind == "A":
            arrived(x_buf.at[s, pl.ds(cap, cap), c], xa_r.at[p, s])
            arrived(x_buf.at[s, pl.ds(group + cap, cap), c], xb_r.at[p, s])
        else:
            arrived(x_buf.at[s, pl.ds(group, group), c], yp_r.at[p, s])
        send(x_buf.at[s, mine, c], x_buf.at[s, pl.ds(2 * group, 2 * group), c],
             cc_s.at[p, s], cc_r.at[p, s], c_peer)

    first_up = next(i for name, _, i in plan if name == "up")
    ups = sum(1 for name, _, i in plan if name == "up" and i == first_up)
    pieces = spans(wg.shape[0], 256)

    def up(p, i):
        s = block_at(i)
        if p == 0:
            for q in range(len(in_parts)):
                arrived(x_buf.at[s, mine, cols(in_parts, q)], cc_r.at[q, s])

            @pl.when(i == first_up)
            def _():
                for load in loads:
                    load.wait()

        across = (((1,), (1,)), ((), ()))
        for low, high in pieces if ups == 1 else pieces[p::ups]:
            block = x_buf[s]
            gate = lax.dot_general(block, wg[low:high, :], across, preferred_element_type=f32)
            more = lax.dot_general(block, wu[low:high, :], across, preferred_element_type=f32)
            hid[:, low:high] = activate(gate, more).astype(bf16)

    def down(p, i):
        s = block_at(i)
        _, start, stop = out_parts[p]
        for low, high in spans(stop - start, 512):
            here = slice(start + low, start + high)
            part[s, :, here] = jnp.dot(
                hid[...], wd[:, here], preferred_element_type=f32
            ).astype(bf16)
        c = cols(out_parts, p)
        send(part.at[s, pl.ds(2 * group, 2 * group), c], c_in.at[s, :, c],
             pc_s.at[p, s], pc_r.at[p, s], c_peer)

    def pair(s, low, count, c):
        return part[s, pl.ds(low, count), c].astype(f32) + c_in[s, pl.ds(low, count), c].astype(f32)

    def core(p, j):
        s = block_at(j)
        kind, c = out_parts[p][0], cols(out_parts, p)
        arrived(c_in.at[s, :, c], pc_r.at[p, s])
        if kind == "A":
            for n in range(2):
                x_out[s, pl.ds(n * cap, cap), c] = pair(s, cap + n * group, cap, c).astype(bf16)
            send(x_out.at[s, :, c], x_in.at[s, :, c], px_s.at[p, s], px_r.at[p, s], x_peer)
        else:
            y_out[s, :, c] = pair(s, group, group, c).astype(bf16)
            send(y_out.at[s, :, c], y_in.at[s, :, c], py_s.at[p, s], py_r.at[p, s], y_peer)

    def detour(source, owner):
        return ((source == 0) & (owner > 1)) | ((source == depth - 1) & (owner < depth - 2))

    def joins(s):
        return ((z == 1) & (s > 1)) | ((z == depth - 2) & (s < depth - 2))

    def z_rows(p):
        return pl.ds(0, 2 * rows if out_parts[p][0] == "C" else rows)

    def z_send(p, s, ready):
        c, r = cols(out_parts, p), z_rows(p)

        @pl.when(ready & detour(z, s))
        def _():
            send(z_out.at[s, r, c], mid_in.at[s, r, c], pz_s.at[p, s], mi_r.at[p, s],
                 z_peer(jnp.where(z == 0, 1, depth - 2)))

        @pl.when(ready & jnp.logical_not(detour(z, s)))
        def _():
            send(z_out.at[s, r, c], z_in.at[z, r, c], pz_s.at[p, s], pz_r.at[p, z], z_peer(s))

    def deliver(p, s, total, far=None):
        c = cols(out_parts, p)

        @pl.when(s == z)
        def _():
            acc[:, c] = total
            if far is not None:
                far_acc[:, c] = far

        @pl.when(s != z)
        def _():
            z_out[s, pl.ds(0, rows), c] = total.astype(bf16)
            if far is not None:
                z_out[s, pl.ds(rows, rows), c] = far.astype(bf16)

        z_send(p, s, (s != z) & jnp.logical_not(joins(s)))

    def far_mix(p, s):
        c = cols(out_parts, p)
        return spread(far_meta[s], pair(s, cap, cap, c).astype(bf16), y_in[s, pl.ds(cap, cap), c])

    def own_mix(p, s):
        c = cols(out_parts, p)
        return spread(meta[s], pair(s, 0, cap, c).astype(bf16), y_in[s, own_slots, c])

    def gather(p, j):
        s = block_at(j)
        kind, c = out_parts[p][0], cols(out_parts, p)
        if kind == "A":
            arrived(x_in.at[s, :, c], px_r.at[p, s])
            y_out[s, own_slots, c] = (
                pair(s, group, cap, c) + x_in[s, pl.ds(cap, cap), c].astype(f32)
            ).astype(bf16)
            send(y_out.at[s, own_slots, c], y_in.at[s, own_slots, c],
                 py_s.at[p, s], py_r.at[p, s], y_peer)
            return
        arrived(y_in.at[s, :, c], py_r.at[p, s])
        if kind == "B":
            x_out[s, pl.ds(0, rows), c] = far_mix(p, s).astype(bf16)
            send(x_out.at[s, pl.ds(0, rows), c], x_in.at[s, pl.ds(0, rows), c],
                 px_s.at[p, s], px_r.at[p, s], x_peer)
        else:
            deliver(p, s, own_mix(p, s), far_mix(p, s))

    def comb(p, j):
        s = block_at(j)
        kind, c = out_parts[p][0], cols(out_parts, p)
        if kind == "A":
            arrived(y_in.at[s, own_slots, c], py_r.at[p, s])
            own = (pair(s, 0, cap, c) + x_in[s, own_slots, c].astype(f32)).astype(bf16)
            deliver(p, s, spread(meta[s], own, y_in[s, own_slots, c]))
        else:
            arrived(x_in.at[s, pl.ds(0, rows), c], px_r.at[p, s])
            deliver(p, s, own_mix(p, s) + x_in[s, pl.ds(0, rows), c].astype(f32))

    def chain(p, j):
        s = block_at(j)
        c, r = cols(out_parts, p), z_rows(p)

        @pl.when(joins(s))
        def _():
            arrived(mid_in.at[s, r, c], mi_r.at[p, s])
            z_out[s, r, c] = (z_out[s, r, c].astype(f32) + mid_in[s, r, c].astype(f32)).astype(bf16)

        z_send(p, s, joins(s))

    table = {
        "meta": greet, "relay": relay, "choose": choose, "forward": forward, "to_core": to_core,
        "up": up, "down": down, "core": core, "sum": gather, "comb": comb, "chain": chain,
    }

    for name, p, i in plan:
        table[name](p, i)

    def settle(s, carry):
        passed(s, meta.at[s], m_s.at[0, s], m_s.at[1, s])
        passed(s, far_meta.at[s], fm_s.at[0, s], fm_s.at[1, s])
        for p, (kind, _, _) in enumerate(in_parts):
            c = cols(in_parts, p)
            passed(s, tok.at[s, :, c], zt_s.at[p, 0, s], zt_s.at[p, 1, s])
            if kind == "C":
                passed(s, far_tok.at[s, :, c], zf_s.at[p, 0, s], zf_s.at[p, 1, s])
            if kind != "A":
                @pl.when((s == z) | (kind == "B"))
                def _():
                    arrived(far_tok.at[s, :, c], raw_s.at[p, s])

                arrived(y_pick.at[s, :, c], yp_s.at[p, s])
            else:
                slab = x_buf.at[s, own_slots, c]
                for sem in (yp_s, xa_s, xb_s):
                    arrived(slab, sem.at[p, s])
            arrived(x_buf.at[s, mine, c], cc_s.at[p, s])
        for p, (kind, _, _) in enumerate(out_parts):
            c = cols(out_parts, p)
            arrived(c_in.at[s, :, c], pc_s.at[p, s])
            if kind == "A":
                arrived(x_out.at[s, :, c], px_s.at[p, s])
                arrived(y_out.at[s, own_slots, c], py_s.at[p, s])
            else:
                arrived(y_out.at[s, :, c], py_s.at[p, s])
                if kind == "B":
                    arrived(x_out.at[s, pl.ds(0, rows), c], px_s.at[p, s])
        return carry

    lax.fori_loop(0, depth, settle, 0)
    arrived(meta.at[0], fx_s.at[0])

    def collect(p):
        kind, c = out_parts[p][0], cols(out_parts, p)
        for step in range(1, depth):
            q = ahead(step)

            @pl.when(jnp.logical_not(detour(q, z)))
            def _():
                arrived(z_in.at[q, z_rows(p), c], pz_r.at[p, q])
                acc[:, c] = acc[:, c] + z_in[q, pl.ds(0, rows), c].astype(f32)
                if kind == "C":
                    far_acc[:, c] = far_acc[:, c] + z_in[q, pl.ds(rows, rows), c].astype(f32)

    def leave(p):
        c = cols(out_parts, p)
        pltpu.make_async_copy(done.at[:, c], out.at[:, c], out_sem.at[p]).start()

    crossing = [p for p, (kind, _, _) in enumerate(out_parts) if kind == "C"]
    for p in crossing:
        c = cols(out_parts, p)
        collect(p)
        last_out[:, c] = far_acc[:, c].astype(bf16)
        send(last_out.at[:, c], last_in.at[:, c], last_s.at[p], last_r.at[p], x_peer)
    for p in range(len(out_parts)):
        if p not in crossing:
            c = cols(out_parts, p)
            collect(p)
            done[:, c] = acc[:, c].astype(bf16)
            leave(p)
    for p in crossing:
        c = cols(out_parts, p)
        arrived(last_in.at[:, c], last_r.at[p])
        done[:, c] = (acc[:, c] + last_in[:, c].astype(f32)).astype(bf16)
        leave(p)

    for p in crossing:
        arrived(last_out.at[:, cols(out_parts, p)], last_s.at[p])

    for step in range(1, depth):
        s = ahead(step)
        for p in range(len(out_parts)):
            arrived(z_out.at[s, z_rows(p), cols(out_parts, p)], pz_s.at[p, s])
    for p in range(len(out_parts)):
        arrived(done.at[:, cols(out_parts, p)], out_sem.at[p])


IN_PARTS = (("A", 0), ("A", 1024), ("C", 2176))
OUT_PARTS = (("A", 0), ("A", 896), ("C", 1920), ("C", 2432))
PLAN = (
    ("meta", 0, 0), ("choose", 0, 0), ("choose", 1, 0), ("choose", 2, 0), ("forward", 0, 0),
    ("relay", 0, 1), ("forward", 1, 0), ("meta", 0, 1), ("choose", 0, 1), ("relay", 1, 1),
    ("to_core", 0, 0), ("to_core", 2, 0), ("relay", 2, 1), ("choose", 1, 1), ("to_core", 1, 0),
    ("meta", 0, 2), ("choose", 2, 1), ("forward", 0, 1), ("relay", 0, 2), ("up", 0, 0),
    ("forward", 1, 1), ("choose", 0, 2), ("up", 1, 0), ("up", 2, 0), ("to_core", 2, 1),
    ("relay", 1, 2), ("choose", 1, 2), ("down", 2, 0), ("to_core", 0, 1), ("meta", 0, 3),
    ("relay", 2, 2), ("choose", 2, 2), ("forward", 0, 2), ("relay", 0, 3), ("choose", 0, 3),
    ("core", 2, 0), ("to_core", 1, 1), ("down", 0, 0), ("down", 1, 0), ("down", 3, 0),
    ("forward", 1, 2), ("relay", 1, 3), ("choose", 1, 3), ("up", 0, 1), ("up", 1, 1),
    ("to_core", 2, 2), ("up", 2, 1), ("to_core", 0, 2), ("down", 3, 1), ("forward", 0, 3),
    ("relay", 2, 3), ("choose", 2, 3), ("to_core", 1, 2), ("down", 0, 1), ("forward", 1, 3),
    ("down", 2, 1), ("core", 3, 1), ("core", 1, 0), ("down", 1, 1), ("up", 0, 2),
    ("to_core", 0, 3), ("up", 1, 2), ("core", 2, 1), ("to_core", 1, 3), ("up", 2, 2),
    ("to_core", 2, 3), ("core", 0, 1), ("down", 2, 2), ("down", 0, 2), ("sum", 3, 1),
    ("down", 3, 2), ("sum", 2, 1), ("core", 2, 2), ("down", 1, 2), ("core", 0, 2), ("up", 0, 3),
    ("up", 1, 3), ("core", 3, 2), ("sum", 0, 1), ("sum", 2, 2), ("core", 1, 2), ("up", 2, 3),
    ("down", 3, 3), ("down", 1, 3), ("sum", 3, 2), ("core", 3, 3), ("down", 2, 3), ("core", 1, 3),
    ("comb", 0, 1), ("chain", 2, 2), ("core", 2, 3), ("down", 0, 3), ("sum", 0, 2), ("sum", 3, 3),
    ("chain", 3, 1), ("sum", 1, 2), ("core", 0, 3), ("core", 0, 0), ("chain", 2, 1),
    ("sum", 2, 0), ("core", 1, 1), ("sum", 2, 3), ("sum", 1, 3), ("comb", 0, 2), ("chain", 3, 3),
    ("sum", 0, 3), ("comb", 1, 3), ("core", 3, 0), ("chain", 3, 2), ("sum", 1, 0),
    ("chain", 2, 3), ("comb", 0, 3), ("chain", 0, 2), ("chain", 0, 1), ("comb", 1, 2),
    ("sum", 0, 0), ("sum", 3, 0), ("chain", 1, 3), ("sum", 1, 1), ("comb", 1, 0), ("chain", 0, 3),
    ("comb", 0, 0), ("comb", 1, 1), ("chain", 1, 1), ("chain", 1, 2),
)


def gathered_plan(tokens, expert_ids, gate_codes, w_gate, w_up, w_down, capacity, expert_count):
    rows, top = expert_ids.shape
    width = tokens.shape[1]
    w_gate, w_up = jnp.swapaxes(w_gate, 1, 2), jnp.swapaxes(w_up, 1, 2)
    part_width = w_gate.shape[1]
    depth = lax.axis_size("expert") // 2
    f32, bf16 = jnp.float32, jnp.bfloat16
    group = 2 * capacity
    vm, dma = pltpu.VMEM, pltpu.SemaphoreType.DMA

    def bounds(parts):
        lows = [low for _, low in parts]
        return [(kind, low, high) for (kind, low), high in zip(parts, lows[1:] + [width])]

    in_parts, out_parts = bounds(IN_PARTS), bounds(OUT_PARTS)
    ins, outs = len(in_parts), len(out_parts)
    two, one = dma((ins, 2, depth)), dma((ins, depth))
    block = vm((depth, group, width), bf16)
    pair = vm((depth, 2 * rows, width), bf16)
    return pl.pallas_call(
        functools.partial(fused, depth, expert_count, capacity, in_parts, out_parts, PLAN),
        out_shape=jax.ShapeDtypeStruct((rows, width), bf16),
        in_specs=[pl.BlockSpec(memory_space=pl.ANY)] * 6,
        out_specs=pl.BlockSpec(memory_space=pl.ANY),
        scratch_shapes=[
            vm((top, rows), jnp.int32),
            vm((top, rows), jnp.int32),
            vm((rows, width), bf16),
            vm((depth, rows, width), bf16),
            vm((depth, rows, width), bf16),
            vm((depth, 2 * expert_count, rows), f32),
            vm((depth, 2 * expert_count, rows), f32),
            block,
            vm((depth, 4 * group, width), bf16),
            vm(w_gate.shape[1:], bf16),
            vm(w_up.shape[1:], bf16),
            vm(w_down.shape[1:], bf16),
            vm((4 * group, part_width), bf16),
            vm((depth, 4 * group, width), bf16),
            vm((depth, 2 * group, width), bf16),
            block,
            block,
            block,
            block,
            pair,
            pair,
            pair,
            vm((rows, width), f32),
            vm((rows, width), f32),
            vm((rows, width), bf16),
            vm((rows, width), bf16),
            dma((6,)),
            dma((outs,)),
            dma((2, depth)),
            dma((depth,)),
            dma((2, depth)),
            dma((depth,)),
            dma((1,)),
            two,
            one,
            two,
        ]
        + [one] * 11
        + [dma((outs, depth))] * 9
        + [dma((outs,))] * 2,
        compiler_params=pltpu.CompilerParams(
            collective_id=0, has_side_effects=True, vmem_limit_bytes=63 << 20
        ),
    )(tokens, expert_ids.T, gate_codes.T, w_gate, w_up, w_down)


def slot_plan(tokens, expert_ids, gate_codes, w_gate, w_up, w_down):
    tok_rows, top_count = expert_ids.shape
    width = tokens.shape[1]
    expert_count = lax.axis_size("expert") * w_gate.shape[0]
    capacity = 3 * tok_rows * top_count // (2 * expert_count)
    slot_count = expert_count * capacity
    flat_ids = expert_ids.reshape(-1)
    onehot = (flat_ids[:, None] == jnp.arange(expert_count, dtype=jnp.int32)[None, :]).astype(
        jnp.int32
    )
    ranking = jnp.sum((jnp.cumsum(onehot, axis=0) - 1) * onehot, axis=1)
    target = flat_ids * capacity + ranking
    picker = (target[:, None] == jnp.arange(slot_count, dtype=jnp.int32)[None, :]).astype(
        jnp.bfloat16
    )
    selector = jnp.sum(picker.reshape(tok_rows, top_count, slot_count), axis=1)
    outgoing = jnp.einsum("ts,td->sd", selector, tokens, preferred_element_type=jnp.float32).astype(
        jnp.bfloat16
    )
    arrived = lax.all_to_all(outgoing, "expert", split_axis=0, concat_axis=0, tiled=True)
    gathered = lax.all_gather(arrived, "replica", axis=0, tiled=True)
    gate = jnp.dot(gathered, w_gate[0], preferred_element_type=jnp.float32)
    up = jnp.dot(gathered, w_up[0], preferred_element_type=jnp.float32)
    hidden = activate(gate, up).astype(jnp.bfloat16)
    summed = lax.psum_scatter(
        jnp.dot(hidden, w_down[0], preferred_element_type=jnp.float32).astype(jnp.bfloat16),
        "replica",
        scatter_dimension=0,
        tiled=True,
    )
    returned = lax.all_to_all(summed, "expert", split_axis=0, concat_axis=0, tiled=True)
    per_choice = jnp.dot(picker, returned, preferred_element_type=jnp.float32)
    gates = gate_codes.astype(jnp.float32) / 65536.0
    weighted = per_choice.reshape(tok_rows, top_count, width) * gates[:, :, None]
    return jnp.sum(weighted, axis=1).astype(jnp.bfloat16)


def on_device(tokens, expert_ids, gate_codes, w_gate, w_up, w_down):
    rows, top = expert_ids.shape
    expert_count = lax.axis_size("expert") * w_gate.shape[0]
    capacity = 3 * rows * top // (2 * expert_count)
    args = (tokens, expert_ids, gate_codes, w_gate, w_up, w_down)
    paired = w_gate.shape[0] == 1 and lax.axis_size("replica") == 2 * CORES
    if paired and 2 * capacity > rows:
        return gathered_plan(*args, capacity, expert_count)
    return slot_plan(*args)


def solution(mesh):
    return jax.shard_map(
        on_device,
        mesh=mesh,
        in_specs=(
            P(("expert", "replica"), None),
            P(("expert", "replica"), None),
            P(("expert", "replica"), None),
            P("expert", None, "replica"),
            P("expert", None, "replica"),
            P("expert", "replica", None),
        ),
        out_specs=P(("expert", "replica"), None),
        check_vma=False,
    )
```
